256 devices in a mesh: seq: 32 (over y, z), tensor: 8 (over x, core).
Axes of the slice: x: 4, y: 4, z: 8, core: 2. Of those that a mesh axis runs over, the one named last changes fastest.
Arguments:
- tokens: int32 [4, 128], replicated, may hold values from 0 to 50175
- lengths: int32 [128], replicated, may hold values from 64 to 3072, as said below
- page_table: int32 [128, 24], replicated, may hold values from -1 to 767, as said below
- embedding: bfloat16 [50176, 2048], P('seq', 'tensor'), may hold values from -24 to 24
- ln1_gain: float32 [2048], replicated, may hold values from 0.5 to 1.5
- ln1_bias: float32 [2048], replicated, may hold values from -3 to 3
- w_query: bfloat16 [2048, 2048], P(None, 'tensor'), may hold values from -0.125 to 0.125
- q_bias: float32 [2048], P('tensor'), may hold values from -3 to 3
- w_key: bfloat16 [2048, 2048], P(None, 'tensor'), may hold values from -0.125 to 0.125
- k_bias: float32 [2048], P('tensor'), may hold values from -3 to 3
- w_value: bfloat16 [2048, 2048], P(None, 'tensor'), may hold values from -0.125 to 0.125
- v_bias: float32 [2048], P('tensor'), may hold values from -3 to 3
- w_out: bfloat16 [2048, 2048], P('tensor'), may hold values from -0.125 to 0.125
- ln2_gain: float32 [2048], replicated, may hold values from 0.5 to 1.5
- ln2_bias: float32 [2048], replicated, may hold values from -3 to 3
- w_gate: bfloat16 [2048, 3072], P(None, 'tensor'), may hold values from -0.125 to 0.125
- w_up: bfloat16 [2048, 3072], P(None, 'tensor'), may hold values from -0.125 to 0.125
- w_down: bfloat16 [3072, 2048], P('tensor'), may hold values from -0.109375 to 0.109375
- k_cache: bfloat16 [768, 128, 2048], P('seq', None, 'tensor'), may hold values from -16 to 16
- v_cache: bfloat16 [768, 128, 2048], P('seq', None, 'tensor'), may hold values from -6 to 6
Outputs:
- output: bfloat16 [4, 128, 2048], P(None, None, 'tensor')
The draws below stay inside these ranges and needn't reach their ends.
Inputs may be any that keep to these rules, and one draw needn't show every extreme that they name: `page_table`: row b lists request b's pages in order: its first ceil(lengths[b] / 128) entries are distinct page numbers, the rest are -1; no page belongs to two requests. All pages of a request lie on one index of seq (page g on index g // 24); every index of seq uses its lowest slots, and some index uses all 24. `lengths`: 8 requests hold more than (23) * 128 positions; every other request holds at most 384.
All inputs are finite; a program needn't handle non-finite values.
Results may differ from the reference program's by a relative error of at most 0.017.
Values may be sent and summed in bfloat16 or wider, within the bound.
A program may use at most 128 MiB of HBM per device.

```python
import math
import jax
import jax.numpy as jnp
import numpy as np
from jax import lax

D = 2048
HEADS = 32
HD = 64
ROT = 16
FF = 3072
V = 50176
PAGE = 128
P_DEV = 24
STEPS = 4
B = 128
LONGS = 8
MAXP = 24
PAGES = 768
QD = 2048
N_TENSOR = 8


def shuffled_slots(slot_key):
    return jax.random.permutation(slot_key, MAXP)


def paging(key):
    device_count = PAGES // P_DEV
    long_count = LONGS
    other_devices = device_count - long_count
    short_count = B - long_count
    split_keys = jax.random.split(jax.random.fold_in(key, 41), 5)
    device_order = jax.random.permutation(split_keys[0], device_count)
    request_order = jax.random.permutation(split_keys[1], B)
    long_lengths = MAXP * PAGE - jax.random.randint(split_keys[2], (long_count,), 0, PAGE)
    long_lengths = long_lengths.at[0].set(MAXP * PAGE)
    short_lengths = jax.random.randint(split_keys[3], (short_count,), PAGE // 2, 3 * PAGE + 1)
    short_lengths = short_lengths.at[0].set(PAGE // 2)
    slot_orders = jax.vmap(shuffled_slots)(jax.random.split(split_keys[4], long_count))
    long_table = device_order[:long_count][:, None] * P_DEV + slot_orders
    short_devices = device_order[long_count + jnp.arange(short_count) % other_devices]
    page_counts = (short_lengths + PAGE - 1) // PAGE
    page_grid = page_counts.reshape(short_count // other_devices, other_devices)
    offsets = (jnp.cumsum(page_grid, axis=0) - page_grid).reshape(-1)
    columns = jnp.arange(MAXP)[None, :]
    short_table = jnp.where(columns < page_counts[:, None], short_devices[:, None] * P_DEV + offsets[:, None] + columns, -1)
    table = jnp.zeros((B, MAXP), jnp.int32)
    table = table.at[request_order[:long_count]].set(long_table.astype(jnp.int32))
    table = table.at[request_order[long_count:]].set(short_table.astype(jnp.int32))
    all_lengths = jnp.zeros((B,), jnp.int32)
    all_lengths = all_lengths.at[request_order[:long_count]].set(long_lengths.astype(jnp.int32))
    all_lengths = all_lengths.at[request_order[long_count:]].set(short_lengths.astype(jnp.int32))
    return (table, all_lengths)


def draw_page_table(key, part):
    return paging(key)[0]


def draw_lengths(key, part):
    return paging(key)[1]


def bias_pattern(key):
    key_drawn = jax.random.fold_in(jax.random.fold_in(key, 23), 0)
    drawn = jnp.clip(0.5 * jax.random.normal(key_drawn, (QD,), jnp.float32), -2.5, 2.5)
    return drawn


def draw_q_bias(key, part):
    drawn = bias_pattern(key)
    return drawn.astype(jnp.float32)


def draw_k_cache(key, part):
    drawn = jnp.clip(jax.random.normal(jax.random.fold_in(key, 29), (PAGES, PAGE, QD), jnp.float32), -4.5, 4.5)
    return drawn.astype(jnp.bfloat16)


def draw_embedding(key, part):
    key_base, key_cols = jax.random.split(jax.random.fold_in(key, 17), 2)
    drawn = jnp.clip(jax.random.normal(key_base, (V, D), jnp.float32), -4.0, 4.0)
    trend = jnp.arange(D, dtype=jnp.float32) / D
    jitter = jax.random.uniform(key_cols, (D,), jnp.float32)
    column_scale = 0.3 * jnp.exp(math.log(10.0) * 0.5 * (trend + jitter))
    return (drawn * column_scale[None, :]).astype(jnp.bfloat16)


def with_ends(values, stream_key, low, top_value):
    place = [jax.random.randint(jax.random.fold_in(stream_key, axis), (), 0, length) for axis, length in enumerate(values.shape)]
    main_axis = values.shape.index(max(values.shape))
    next_to = place[:main_axis] + [(place[main_axis] + 1) % values.shape[main_axis]] + place[main_axis + 1:]
    return values.at[tuple(place)].set(low).at[tuple(next_to)].set(top_value)


def shard_levels(own_key, extent, cuts, least, largest):
    gain, own = 1.0, jax.random.fold_in(own_key, 6)
    for axis_at, blocks in cuts:
        heights = jnp.exp(jax.random.uniform(jax.random.fold_in(own, axis_at), (blocks,), jnp.float32, least / len(cuts), largest / len(cuts)))
        gain = gain * jnp.repeat(heights, extent[axis_at] // blocks).reshape([-1 if axis == axis_at else 1 for axis in range(len(extent))])
    return gain


def cumulative_ranks(amount, skew):
    loads = [(1 << 20) // math.isqrt(rank ** skew) + 1 for rank in range(1, amount + 1)]
    width = 1 + sum(loads) // (1 << 30)
    return np.cumsum(np.array([max(1, weight // width) for weight in loads]))


def skewed_ids(rng, extent, amount, skew):
    table = cumulative_ranks(amount, skew)
    pick = jax.random.randint(jax.random.fold_in(rng, 1), extent, 0, int(table[amount - 1]))
    standing = jnp.searchsorted(jnp.asarray(table, jnp.int32), pick, side="right")
    return jax.random.permutation(jax.random.fold_in(rng, 2), amount)[standing].astype(jnp.int32)


def centred(own_key, dims, spread, bound, cuts=(), kind=jnp.bfloat16):
    entries = jax.random.normal(own_key, dims, jnp.float32) * spread
    if len(cuts) > 0:
        entries = shard_levels(own_key, dims, cuts, -0.22, 0.18) * entries
    return jnp.clip(entries, min=-bound, max=bound).astype(kind)


def setup_inputs(seed: int = 0) -> dict:
    key_list = jax.random.split(jax.random.key(seed), 21)
    tokens = with_ends(skewed_ids(key_list[0], (STEPS, B), V, 2), jax.random.fold_in(key_list[0], 3), 0, V - 1).astype(jnp.int32)
    lengths = draw_lengths(jax.random.fold_in(key_list[20], 71), 0)
    page_table = draw_page_table(jax.random.fold_in(key_list[20], 71), 0)
    embedding = draw_embedding(jax.random.fold_in(key_list[20], 71), 0)
    ln1_gain = jnp.clip(1.0 + 0.1 * jax.random.normal(key_list[4], (D,), jnp.float32), 0.5, 1.5)
    ln1_bias = centred(key_list[5], (D,), 0.5, 3.0, (), jnp.float32)
    w_query = centred(key_list[6], (D, QD), D ** -0.5, 0.125, ((1, 8),))
    q_bias = draw_q_bias(jax.random.fold_in(key_list[20], 71), 0)
    w_key = centred(key_list[8], (D, QD), D ** -0.5, 0.125, ((1, 8),))
    k_bias = centred(key_list[9], (QD,), 0.5, 3.0, ((0, 8),), jnp.float32)
    w_value = centred(key_list[10], (D, QD), D ** -0.5, 0.125, ((1, 8),))
    v_bias = centred(key_list[11], (QD,), 0.5, 3.0, ((0, 8),), jnp.float32)
    w_out = centred(key_list[12], (QD, D), QD ** -0.5, 0.125, ((0, 8),))
    ln2_gain = jnp.clip(1.0 + 0.1 * jax.random.normal(key_list[13], (D,), jnp.float32), 0.5, 1.5)
    ln2_bias = centred(key_list[14], (D,), 0.5, 3.0, (), jnp.float32)
    w_gate = centred(key_list[15], (D, FF), D ** -0.5, 0.125, ((1, 8),))
    w_up = centred(key_list[16], (D, FF), D ** -0.5, 0.125, ((1, 8),))
    w_down = centred(key_list[17], (FF, D), FF ** -0.5, 0.109375, ((0, 8),))
    k_cache = draw_k_cache(jax.random.fold_in(key_list[20], 71), 0)
    v_cache = centred(key_list[19], (PAGES, PAGE, QD), 1.0, 6.0, ((0, 32), (2, 8)))
    return {"tokens": tokens, "lengths": lengths, "page_table": page_table, "embedding": embedding, "ln1_gain": ln1_gain, "ln1_bias": ln1_bias, "w_query": w_query, "q_bias": q_bias, "w_key": w_key, "k_bias": k_bias, "w_value": w_value, "v_bias": v_bias, "w_out": w_out, "ln2_gain": ln2_gain, "ln2_bias": ln2_bias, "w_gate": w_gate, "w_up": w_up, "w_down": w_down, "k_cache": k_cache, "v_cache": v_cache}


EPSILON = 1e-05
NEGATIVE = -1e+30
THETA = 10000.0

def rotary(field, positions, rotated):
    half_rot = rotated // 2
    frequency = THETA ** (-(jnp.arange(half_rot, dtype=jnp.float32) * 2.0) / rotated)
    angles = positions.astype(jnp.float32)[:, None] * frequency[None, :]
    cosine = jnp.concatenate([jnp.cos(angles), jnp.cos(angles)], -1)[:, None, :]
    sine_part = jnp.concatenate([jnp.sin(angles), jnp.sin(angles)], -1)[:, None, :]
    leading = field[..., :rotated]
    turned = jnp.concatenate([-leading[..., half_rot:], leading[..., :half_rot]], -1)
    return jnp.concatenate([leading * cosine + turned * sine_part, field[..., rotated:]], -1)

def norm_full(inputs, norm_gain, norm_bias):
    values = inputs.astype(jnp.float32)
    average = lax.optimization_barrier(jnp.mean(values, -1, keepdims=True))
    squares = lax.optimization_barrier(jnp.mean(values * values, -1, keepdims=True))
    inverse = lax.rsqrt(squares - average * average + EPSILON)
    return ((values - average) * inverse * norm_gain + norm_bias).astype(jnp.bfloat16)

def grouped_product(left_side, right_side, groups):
    share_rows = right_side.shape[0] // groups
    result = jnp.zeros((left_side.shape[0], right_side.shape[1]), jnp.float32)
    for group_number in range(groups):
        low_edge = group_number * share_rows
        term_part = jnp.dot(left_side[:, low_edge:low_edge + share_rows], right_side[low_edge:low_edge + share_rows], preferred_element_type=jnp.float32).astype(jnp.bfloat16)
        result = result + lax.optimization_barrier(term_part).astype(jnp.float32)
    return result

def reference(tokens, lengths, page_table, embedding, ln1_gain, ln1_bias, w_query, q_bias, w_key, k_bias, w_value, v_bias, w_out, ln2_gain, ln2_bias, w_gate, w_up, w_down, k_cache, v_cache):
    step_count, requests = tokens.shape
    row_count = step_count * requests
    scale_factor = HD ** (-0.5)
    residual = jnp.take(embedding, tokens.reshape(-1), axis=0)
    normed = norm_full(residual, ln1_gain, ln1_bias)
    positions = (lengths[None, :] + jnp.arange(step_count, dtype=jnp.int32)[:, None]).reshape(-1)
    queries = rotary((jnp.dot(normed, w_query, preferred_element_type=jnp.float32) + q_bias).reshape(row_count, HEADS, HD), positions, ROT).astype(jnp.bfloat16)
    new_keys = rotary((jnp.dot(normed, w_key, preferred_element_type=jnp.float32) + k_bias).reshape(row_count, HEADS, HD), positions, ROT).astype(jnp.bfloat16)
    new_values = (jnp.dot(normed, w_value, preferred_element_type=jnp.float32) + v_bias).reshape(row_count, HEADS, HD).astype(jnp.bfloat16)

    def by_request(field):
        return field.reshape(step_count, requests, HEADS, HD).transpose(1, 0, 2, 3)
    causal = jnp.arange(step_count)[None, :] <= jnp.arange(step_count)[:, None]
    slot_spots = jnp.arange(MAXP, dtype=jnp.int32)[:, None] * PAGE + jnp.arange(PAGE, dtype=jnp.int32)[None, :]

    def attend_one(packed):
        query_one, key_one, value_one, table_row, length_one = packed
        page_ids = jnp.maximum(table_row, 0)
        page_keys = jnp.take(k_cache, page_ids, axis=0).reshape(MAXP, PAGE, HEADS, HD).astype(jnp.float32)
        page_values = jnp.take(v_cache, page_ids, axis=0).reshape(MAXP, PAGE, HEADS, HD).astype(jnp.float32)
        scores = jnp.einsum('qhd,jphd->jqhp', query_one.astype(jnp.float32), page_keys) * scale_factor
        visible = (slot_spots < length_one) & (table_row[:, None] >= 0)
        scores = jnp.where(visible[:, None, None, :], scores, NEGATIVE)
        page_top = lax.optimization_barrier(jnp.max(scores, -1))
        rounded = jnp.where(visible[:, None, None, :], jnp.exp(scores - page_top[..., None]), 0.0).astype(jnp.bfloat16)
        weights = lax.optimization_barrier(rounded).astype(jnp.float32)
        page_mass = lax.optimization_barrier(jnp.sum(weights, -1))
        page_mix = jnp.einsum('jqhp,jphd->jqhd', weights, page_values)
        fresh_scores = jnp.einsum('qhd,khd->qhk', query_one.astype(jnp.float32), key_one.astype(jnp.float32)) * scale_factor
        fresh_scores = jnp.where(causal[:, None, :], fresh_scores, NEGATIVE)
        fresh_top = lax.optimization_barrier(jnp.max(fresh_scores, -1))
        fresh_rounded = jnp.where(causal[:, None, :], jnp.exp(fresh_scores - fresh_top[..., None]), 0.0).astype(jnp.bfloat16)
        fresh_weights = lax.optimization_barrier(fresh_rounded).astype(jnp.float32)
        fresh_mass = lax.optimization_barrier(jnp.sum(fresh_weights, -1))
        fresh_mix = jnp.einsum('qhk,khd->qhd', fresh_weights, value_one.astype(jnp.float32))
        overall = jnp.maximum(lax.optimization_barrier(jnp.max(page_top, 0)), fresh_top)
        page_factor = jnp.exp(page_top - overall[None])
        fresh_factor = jnp.exp(fresh_top - overall)
        total_mass = lax.optimization_barrier(jnp.sum(page_mass * page_factor, 0)) + fresh_mass * fresh_factor
        total_mix = lax.optimization_barrier(jnp.sum(page_mix * page_factor[..., None], 0)) + fresh_mix * fresh_factor[..., None]
        return (total_mix / total_mass[..., None]).astype(jnp.bfloat16)
    attended = lax.map(attend_one, (by_request(queries), by_request(new_keys), by_request(new_values), page_table, lengths))
    attn_rows = attended.transpose(1, 0, 2, 3).reshape(row_count, HEADS * HD)
    attn_total = grouped_product(attn_rows, w_out, N_TENSOR)
    hidden_one = (residual.astype(jnp.float32) + attn_total).astype(jnp.bfloat16)
    normed_two = norm_full(hidden_one, ln2_gain, ln2_bias)
    gate_part = jnp.dot(normed_two, w_gate, preferred_element_type=jnp.float32)
    up_part = jnp.dot(normed_two, w_up, preferred_element_type=jnp.float32)
    activated = (jax.nn.silu(gate_part) * up_part).astype(jnp.bfloat16)
    mlp_total = grouped_product(activated, w_down, N_TENSOR)
    output = (hidden_one.astype(jnp.float32) + mlp_total).astype(jnp.bfloat16)
    return output.reshape(step_count, requests, -1)
```

```python
import functools

import jax
import jax.numpy as jnp
from jax import lax
from jax.experimental import pallas as pl
from jax.experimental.pallas import tpu as pltpu
from jax.sharding import PartitionSpec as P

HD = 64
ROT = 16
EPSILON = 1e-05
NEGATIVE = -1e30
THETA = 10000.0
MESH = pl.DeviceIdType.MESH
F32 = jnp.float32
BF16 = jnp.bfloat16


def iota(shape, axis):
    return lax.broadcasted_iota(jnp.int32, shape, axis)


def dot(left, right):
    return jnp.dot(left, right, preferred_element_type=F32)


def dot_nt(left, right):
    return lax.dot_general(left, right, (((1,), (1,)), ((), ())), preferred_element_type=F32)


def layer_kernel(
    n_seq,
    n_ten,
    tok_ref,
    cos_ref,
    sin_ref,
    posown_ref,
    rowcol_ref,
    rowrow_ref,
    g1_ref,
    b1_ref,
    qb_ref,
    kb_ref,
    vb_ref,
    g2_ref,
    b2_ref,
    emb_hbm,
    wq_hbm,
    wk_hbm,
    wv_hbm,
    wo_hbm,
    wg_hbm,
    wu_hbm,
    wd_hbm,
    kc_hbm,
    vc_hbm,
    out_ref,
    emb,
    wq,
    wk,
    wv,
    wo,
    wg,
    wu,
    wd,
    kc,
    vc,
    send_a,
    recv_a,
    res_own,
    res_all,
    nrm,
    q_own,
    q_all,
    q_rows,
    sbuf,
    xbuf,
    send_c,
    recv_c,
    send_e,
    recv_e,
    h1_own,
    h1_all,
    send_h,
    recv_h,
    out_own,
    out_all,
    load_sem,
    send_sem,
    recv_sem,
):
    me = lax.axis_index("seq")
    mt = lax.axis_index("tensor")
    rows_own, cols = q_own.shape
    heads = cols // HD
    slots, page = kc.shape[0], kc.shape[1]
    rows_all = n_seq * rows_own
    width = n_ten * cols

    loads = []
    for index, (source, target) in enumerate(
        (
            (emb_hbm, emb),
            (wq_hbm, wq),
            (wk_hbm, wk),
            (wv_hbm, wv),
            (kc_hbm, kc),
            (vc_hbm, vc),
            (wo_hbm, wo),
            (wg_hbm, wg),
            (wu_hbm, wu),
            (wd_hbm, wd),
        )
    ):
        copy = pltpu.make_async_copy(source, target, load_sem.at[index])
        copy.start()
        loads.append(copy)

    barrier = pltpu.get_barrier_semaphore()

    @pl.loop(1, n_seq)
    def _(step):
        pl.semaphore_signal(
            barrier, inc=1, device_id=(lax.rem(me + step, n_seq), mt), device_id_type=MESH
        )

    @pl.loop(1, n_ten)
    def _(step):
        pl.semaphore_signal(
            barrier, inc=1, device_id=(me, lax.rem(mt + step, n_ten)), device_id_type=MESH
        )

    def all_to_all(stage, over_seq, source, target):
        count = n_seq if over_seq else n_ten

        @pl.loop(1, count)
        def _(step):
            if over_seq:
                peer = lax.rem(me + step, n_seq)
                device = (peer, mt)
            else:
                peer = lax.rem(mt + step, n_ten)
                device = (me, peer)
            pltpu.make_async_remote_copy(
                src_ref=source.at[peer],
                dst_ref=target.at[step - 1],
                send_sem=send_sem.at[stage],
                recv_sem=recv_sem.at[stage],
                device_id=device,
                device_id_type=MESH,
            ).start()

    def spread(stage, over_seq, source, target):
        count = n_seq if over_seq else n_ten
        own = me if over_seq else mt

        @pl.loop(1, count)
        def _(step):
            if over_seq:
                device = (lax.rem(me + step, n_seq), mt)
            else:
                device = (me, lax.rem(mt + step, n_ten))
            pltpu.make_async_remote_copy(
                src_ref=source,
                dst_ref=target.at[own],
                send_sem=send_sem.at[stage],
                recv_sem=recv_sem.at[stage],
                device_id=device,
                device_id_type=MESH,
            ).start()

    def arrived(stage, over_seq, target):
        part = target.at[pl.ds(0, (n_seq if over_seq else n_ten) - 1)]
        pltpu.make_async_copy(part, part, recv_sem.at[stage]).wait()

    def departed(stage, over_seq, target):
        part = target.at[pl.ds(0, (n_seq if over_seq else n_ten) - 1)]
        pltpu.make_async_copy(part, part, send_sem.at[stage]).wait()

    def normalise(blocks, gain, bias):
        total = jnp.zeros((rows_own, 1), F32)
        square = jnp.zeros((rows_own, 1), F32)
        for c in range(n_ten):
            part = blocks[c].astype(F32)
            total += jnp.sum(part, -1, keepdims=True)
            square += jnp.sum(part * part, -1, keepdims=True)
        average = total / width
        inverse = lax.rsqrt(square / width - average * average + EPSILON)
        for c in range(n_ten):
            at = slice(c * cols, (c + 1) * cols)
            part = blocks[c].astype(F32)
            nrm[:, at] = ((part - average) * inverse * gain[:, at] + bias[:, at]).astype(BF16)

    loads[0].wait()
    vocab = emb.shape[0]
    tile_rows = min(rows_all, 128)
    for tile in range(rows_all // tile_rows):
        at = slice(tile * tile_rows, (tile + 1) * tile_rows)
        hit = tok_ref[at, :] == iota((tile_rows, vocab), 1)
        looked = dot(jnp.where(hit, 1.0, 0.0).astype(BF16), emb[...])
        blocks = tile_rows // rows_own
        send_a[tile * blocks : (tile + 1) * blocks] = looked.astype(BF16).reshape(
            blocks, rows_own, cols
        )

    pl.semaphore_wait(barrier, n_seq + n_ten - 2)
    all_to_all(0, True, send_a, recv_a)
    own_part = send_a[me].astype(F32)
    arrived(0, True, recv_a)
    residual = own_part + jnp.sum(recv_a[...].astype(F32), 0)
    res_own[...] = residual.astype(BF16)
    spread(1, False, res_own, res_all)
    res_all[mt] = residual.astype(BF16)
    arrived(1, False, res_all)
    normalise(res_all, g1_ref, b1_ref)

    lane = iota((rows_own, cols), 1)
    first_half = (lane % HD) < (ROT // 2)

    def rotated(field):
        partner = jnp.where(
            first_half,
            pltpu.roll(field, cols - ROT // 2, 1),
            pltpu.roll(field, ROT // 2, 1),
        )
        return field * cos_ref[...] + partner * sin_ref[...]

    loads[1].wait()
    queries = rotated(dot(nrm[...], wq[...]) + qb_ref[...]).astype(BF16)
    q_own[...] = queries
    spread(2, True, q_own, q_all)
    q_all[me] = queries
    loads[2].wait()
    loads[3].wait()
    new_keys = rotated(dot(nrm[...], wk[...]) + kb_ref[...]).astype(BF16)
    new_values = (dot(nrm[...], wv[...]) + vb_ref[...]).astype(BF16)

    steps = 4
    scale = HD**-0.5
    head_of = lane // HD
    q_tall = jnp.concatenate(
        [jnp.where(head_of == h, queries, jnp.zeros_like(queries)) for h in range(heads)], 0
    )
    tall = (heads * rows_own, rows_own)
    query_row = iota(tall, 0) % rows_own
    key_row = iota(tall, 1)
    seen = (query_row // steps == key_row // steps) & (key_row <= query_row)
    fresh = jnp.where(seen, dot_nt(q_tall, new_keys) * scale, NEGATIVE)
    fresh_top = jnp.max(fresh, -1, keepdims=True)
    fresh_weights = jnp.where(seen, jnp.exp(fresh - fresh_top), 0.0).astype(BF16)
    fresh_mass = jnp.sum(fresh_weights.astype(F32), -1, keepdims=True)
    fresh_mix = dot(fresh_weights, new_values)
    top_wide = jnp.zeros((rows_own, cols), F32)
    mass_wide = jnp.zeros((rows_own, cols), F32)
    mix_wide = jnp.zeros((rows_own, cols), F32)
    for h in range(heads):
        at = slice(h * rows_own, (h + 1) * rows_own)
        top_wide = jnp.where(head_of == h, fresh_top[at], top_wide)
        mass_wide = jnp.where(head_of == h, fresh_mass[at], mass_wide)
        mix_wide = jnp.where(head_of == h, fresh_mix[at], mix_wide)

    rows_slot = slots * steps * heads
    row_code = rowcol_ref[...]
    arrived(2, True, q_all)
    pick = jnp.where(row_code == iota((rows_slot, rows_all), 1), 1.0, 0.0).astype(BF16)
    picked = dot(pick, q_all[...].reshape(rows_all, cols))
    row_head = iota((rows_slot, cols), 0) % heads
    own_head = row_head == iota((rows_slot, cols), 1) // HD
    q_rows[...] = jnp.where(own_head, picked, 0.0).astype(BF16)
    row_owner = row_code - (iota((rows_slot, 1), 0) // heads) % steps
    group = 4 if slots % 4 == 0 else 1
    span = group * page
    loads[4].wait()
    top = jnp.full((rows_slot, 1), NEGATIVE, F32)
    for g in range(slots // group):
        at = slice(g * span, (g + 1) * span)
        keys = kc[g * group : (g + 1) * group].reshape(span, cols)
        scores = dot_nt(q_rows[...], keys) * scale
        scores = jnp.where(row_owner == posown_ref[:, at], scores, NEGATIVE)
        sbuf[:, at] = scores
        top = jnp.maximum(top, jnp.max(scores, -1, keepdims=True))
    loads[5].wait()
    mass = jnp.zeros((rows_slot, 1), F32)
    mix = jnp.zeros((rows_slot, cols), F32)
    for g in range(slots // group):
        at = slice(g * span, (g + 1) * span)
        weights = jnp.exp(sbuf[:, at] - top).astype(BF16)
        mass += jnp.sum(weights.astype(F32), -1, keepdims=True)
        mix += dot(weights, vc[g * group : (g + 1) * group].reshape(span, cols))
    level = top + jnp.log(mass)
    high = level.astype(BF16).astype(F32)
    middle = (level - high).astype(BF16).astype(F32)
    low = level - high - middle
    xbuf[:, :cols] = jnp.where(own_head, mix / mass, 0.0).astype(BF16)
    extra = xbuf.shape[1] - cols
    place = iota((rows_slot, extra), 1)
    head_col = iota((rows_slot, extra), 0) % heads
    parts = jnp.where(place == head_col, high, 0.0)
    parts = jnp.where(place == head_col + heads, middle, parts)
    parts = jnp.where(place == head_col + 2 * heads, low, parts)
    xbuf[:, cols:] = parts.astype(BF16)
    put = jnp.where(rowrow_ref[...] == iota((rows_all, rows_slot), 0), 1.0, 0.0).astype(BF16)
    send_c[...] = dot(put, xbuf[...]).astype(BF16).reshape(n_seq, rows_own, cols + extra)
    all_to_all(3, True, send_c, recv_c)
    own_part = send_c[me].astype(F32)
    arrived(3, True, recv_c)
    returned = own_part + jnp.sum(recv_c[...].astype(F32), 0)
    lift = iota((extra, cols), 0)
    lift = jnp.where(
        (lift < 3 * heads) & (lift % heads == iota((extra, cols), 1) // HD), 1.0, 0.0
    ).astype(BF16)
    page_level = dot(returned[:, cols:].astype(BF16), lift)
    overall = jnp.maximum(page_level, top_wide)
    page_factor = jnp.exp(page_level - overall)
    fresh_factor = jnp.exp(top_wide - overall)
    attended = (returned[:, :cols] * page_factor + mix_wide * fresh_factor) / (
        page_factor + mass_wide * fresh_factor
    )

    loads[6].wait()
    partial = dot(attended.astype(BF16), wo[...]).astype(BF16)
    for c in range(n_ten):
        send_e[c] = partial[:, c * cols : (c + 1) * cols]
    all_to_all(4, False, send_e, recv_e)
    own_part = send_e[mt].astype(F32)
    arrived(4, False, recv_e)
    attn_total = own_part + jnp.sum(recv_e[...].astype(F32), 0)
    hidden_one = (residual + attn_total).astype(BF16)
    h1_own[...] = hidden_one
    spread(5, False, h1_own, h1_all)
    h1_all[mt] = hidden_one
    arrived(5, False, h1_all)
    normalise(h1_all, g2_ref, b2_ref)
    loads[7].wait()
    loads[8].wait()
    gate = dot(nrm[...], wg[...])
    up = dot(nrm[...], wu[...])
    activated = (gate / (1.0 + jnp.exp(-gate)) * up).astype(BF16)
    loads[9].wait()
    partial = dot(activated, wd[...]).astype(BF16)
    for c in range(n_ten):
        send_h[c] = partial[:, c * cols : (c + 1) * cols]
    all_to_all(6, False, send_h, recv_h)
    own_part = send_h[mt].astype(F32)
    arrived(6, False, recv_h)
    mlp_total = own_part + jnp.sum(recv_h[...].astype(F32), 0)
    output = (hidden_one.astype(F32) + mlp_total).astype(BF16)
    out_own[...] = output
    spread(7, True, out_own, out_all)
    out_all[me] = output
    departed(0, True, recv_a)
    departed(1, False, res_all)
    departed(2, True, q_all)
    departed(3, True, recv_c)
    departed(4, False, recv_e)
    departed(5, False, h1_all)
    departed(6, False, recv_h)
    arrived(7, True, out_all)
    out_ref[...] = out_all[...]
    departed(7, True, out_all)


def shards(
    n_seq,
    n_ten,
    tokens,
    lengths,
    page_table,
    embedding,
    ln1_gain,
    ln1_bias,
    w_query,
    q_bias,
    w_key,
    k_bias,
    w_value,
    v_bias,
    w_out,
    ln2_gain,
    ln2_bias,
    w_gate,
    w_up,
    w_down,
    k_cache,
    v_cache,
):
    steps, requests = tokens.shape
    rows_all = steps * requests
    rows_own = rows_all // n_seq
    requests_own = requests // n_seq
    slots, page, cols = k_cache.shape
    heads = cols // HD
    width = n_ten * cols
    me = lax.axis_index("seq")
    tok = (tokens - me * embedding.shape[0]).T.reshape(rows_all, 1)

    own_lengths = lax.dynamic_slice_in_dim(lengths, me * requests_own, requests_own, 0)
    positions = (own_lengths[:, None] + jnp.arange(steps, dtype=jnp.int32)[None, :]).reshape(-1)
    half_rot = ROT // 2
    frequency = THETA ** (-(jnp.arange(half_rot, dtype=F32) * 2.0) / ROT)
    angles = positions.astype(F32)[:, None] * frequency[None, :]
    cosine, sine = jnp.cos(angles), jnp.sin(angles)
    rest = HD - ROT
    cos_wide = jnp.tile(
        jnp.concatenate([cosine, cosine, jnp.ones((rows_own, rest), F32)], -1), (1, heads)
    )
    sin_wide = jnp.tile(
        jnp.concatenate([-sine, sine, jnp.zeros((rows_own, rest), F32)], -1), (1, heads)
    )

    matched = page_table[:, :, None] == me * slots + jnp.arange(slots, dtype=jnp.int32)
    request_code = jnp.arange(requests, dtype=jnp.int32)[:, None, None] * steps
    owner = jnp.sum(jnp.where(matched, request_code, 0), (0, 1))
    left = lengths[:, None] - jnp.arange(page_table.shape[1], dtype=jnp.int32) * page
    filled = jnp.sum(jnp.where(matched, jnp.clip(left, 0, page)[:, :, None], 0), (0, 1))
    leads = jnp.any(matched[:, 0], 0)
    spot = jnp.arange(page, dtype=jnp.int32)
    posown = jnp.where(spot < filled[:, None], owner[:, None], -8).reshape(1, slots * page)
    code = jnp.where(
        leads[:, None], owner[:, None] + jnp.arange(steps, dtype=jnp.int32), -1
    )
    code = jnp.broadcast_to(code[:, :, None], (slots, steps, heads)).reshape(-1)
    rows_slot = slots * steps * heads

    vmem = pl.BlockSpec(memory_space=pltpu.VMEM)
    hbm = pl.BlockSpec(memory_space=pl.ANY)
    extra = 128
    scratch = lambda *shape: pltpu.VMEM(shape, BF16)
    out = pl.pallas_call(
        functools.partial(layer_kernel, n_seq, n_ten),
        out_shape=jax.ShapeDtypeStruct((n_seq, rows_own, cols), BF16),
        in_specs=[vmem] * 13 + [hbm] * 10,
        out_specs=vmem,
        scratch_shapes=[
            scratch(*embedding.shape),
            scratch(*w_query.shape),
            scratch(*w_key.shape),
            scratch(*w_value.shape),
            scratch(*w_out.shape),
            scratch(*w_gate.shape),
            scratch(*w_up.shape),
            scratch(*w_down.shape),
            scratch(*k_cache.shape),
            scratch(*v_cache.shape),
            scratch(n_seq, rows_own, cols),
            scratch(n_seq - 1, rows_own, cols),
            scratch(rows_own, cols),
            scratch(n_ten, rows_own, cols),
            scratch(rows_own, width),
            scratch(rows_own, cols),
            scratch(n_seq, rows_own, cols),
            scratch(rows_slot, cols),
            pltpu.VMEM((rows_slot, slots * page), F32),
            scratch(rows_slot, cols + extra),
            scratch(n_seq, rows_own, cols + extra),
            scratch(n_seq - 1, rows_own, cols + extra),
            scratch(n_ten, rows_own, cols),
            scratch(n_ten - 1, rows_own, cols),
            scratch(rows_own, cols),
            scratch(n_ten, rows_own, cols),
            scratch(n_ten, rows_own, cols),
            scratch(n_ten - 1, rows_own, cols),
            scratch(rows_own, cols),
            scratch(n_seq, rows_own, cols),
            pltpu.SemaphoreType.DMA((10,)),
            pltpu.SemaphoreType.DMA((8,)),
            pltpu.SemaphoreType.DMA((8,)),
        ],
        compiler_params=pltpu.CompilerParams(
            collective_id=0, has_side_effects=True, vmem_limit_bytes=62 * 1024 * 1024
        ),
        name="layer",
    )(
        tok,
        cos_wide,
        sin_wide,
        posown,
        code[:, None],
        code[None, :],
        ln1_gain[None],
        ln1_bias[None],
        q_bias[None],
        k_bias[None],
        v_bias[None],
        ln2_gain[None],
        ln2_bias[None],
        embedding,
        w_query,
        w_key,
        w_value,
        w_out,
        w_gate,
        w_up,
        w_down,
        k_cache,
        v_cache,
    )
    out = out.reshape(requests, steps, cols)
    return out.transpose(1, 0, 2)


def solution(mesh):
    placed = (
        P(),
        P(),
        P(),
        P("seq", "tensor"),
        P(),
        P(),
        P(None, "tensor"),
        P("tensor"),
        P(None, "tensor"),
        P("tensor"),
        P(None, "tensor"),
        P("tensor"),
        P("tensor", None),
        P(),
        P(),
        P(None, "tensor"),
        P(None, "tensor"),
        P("tensor", None),
        P("seq", None, "tensor"),
        P("seq", None, "tensor"),
    )
    return jax.shard_map(
        functools.partial(shards, mesh.shape["seq"], mesh.shape["tensor"]),
        mesh=mesh,
        in_specs=placed,
        out_specs=P(None, None, "tensor"),
        check_vma=False,
    )
```

```python
import functools

import jax
import jax.numpy as jnp
from jax import lax
from jax.experimental import pallas as pl
from jax.experimental.pallas import tpu as pltpu
from jax.sharding import PartitionSpec as P

HD = 64
ROT = 16
EPSILON = 1e-05
NEGATIVE = -1e30
THETA = 10000.0
MESH = pl.DeviceIdType.MESH
F32 = jnp.float32
BF16 = jnp.bfloat16


def iota(shape, axis):
    return lax.broadcasted_iota(jnp.int32, shape, axis)


def dot(left, right):
    return jnp.dot(left, right, preferred_element_type=F32)


def dot_nt(left, right):
    return lax.dot_general(left, right, (((1,), (1,)), ((), ())), preferred_element_type=F32)


def layer_kernel(
    n_seq,
    n_ten,
    tok_ref,
    len_ref,
    table_ref,
    g1_ref,
    b1_ref,
    qb_ref,
    kb_ref,
    vb_ref,
    g2_ref,
    b2_ref,
    emb_hbm,
    wq_hbm,
    wk_hbm,
    wv_hbm,
    wo_hbm,
    wg_hbm,
    wu_hbm,
    wd_hbm,
    kc_hbm,
    vc_hbm,
    out_ref,
    emb,
    wq,
    wk,
    wv,
    wo,
    wg,
    wu,
    wd,
    kc,
    vc,
    send_a,
    recv_a,
    res_own,
    res_all,
    nrm,
    q_own,
    q_all,
    q_rows,
    sbuf,
    xbuf,
    send_c,
    recv_c,
    send_e,
    recv_e,
    h1_own,
    h1_all,
    send_h,
    recv_h,
    out_own,
    out_all,
    posown,
    pick,
    put,
    turn,
    load_sem,
    send_sem,
    recv_sem,
):
    me = lax.axis_index("seq")
    mt = lax.axis_index("tensor")
    rows_own, cols = q_own.shape
    heads = cols // HD
    slots, page = kc.shape[0], kc.shape[1]
    rows_all = n_seq * rows_own
    width = n_ten * cols

    loads = []
    for index, (source, target) in enumerate(
        (
            (emb_hbm, emb),
            (wq_hbm, wq),
            (wk_hbm, wk),
            (wv_hbm, wv),
            (kc_hbm, kc),
            (vc_hbm, vc),
            (wo_hbm, wo),
            (wg_hbm, wg),
            (wu_hbm, wu),
            (wd_hbm, wd),
        )
    ):
        copy = pltpu.make_async_copy(source, target, load_sem.at[index])
        copy.start()
        loads.append(copy)

    barrier = pltpu.get_barrier_semaphore()

    @pl.loop(1, n_seq)
    def _(step):
        pl.semaphore_signal(
            barrier, inc=1, device_id=(lax.rem(me + step, n_seq), mt), device_id_type=MESH
        )

    @pl.loop(1, n_ten)
    def _(step):
        pl.semaphore_signal(
            barrier, inc=1, device_id=(me, lax.rem(mt + step, n_ten)), device_id_type=MESH
        )

    def all_to_all(stage, over_seq, source, target):
        count = n_seq if over_seq else n_ten

        @pl.loop(1, count)
        def _(step):
            if over_seq:
                peer = lax.rem(me + step, n_seq)
                device = (peer, mt)
            else:
                peer = lax.rem(mt + step, n_ten)
                device = (me, peer)
            pltpu.make_async_remote_copy(
                src_ref=source.at[peer],
                dst_ref=target.at[step - 1],
                send_sem=send_sem.at[stage],
                recv_sem=recv_sem.at[stage],
                device_id=device,
                device_id_type=MESH,
            ).start()

    def spread(stage, over_seq, source, target):
        count = n_seq if over_seq else n_ten
        own = me if over_seq else mt

        @pl.loop(1, count)
        def _(step):
            if over_seq:
                device = (lax.rem(me + step, n_seq), mt)
            else:
                device = (me, lax.rem(mt + step, n_ten))
            pltpu.make_async_remote_copy(
                src_ref=source,
                dst_ref=target.at[own],
                send_sem=send_sem.at[stage],
                recv_sem=recv_sem.at[stage],
                device_id=device,
                device_id_type=MESH,
            ).start()

    def arrived(stage, over_seq, target):
        part = target.at[pl.ds(0, (n_seq if over_seq else n_ten) - 1)]
        pltpu.make_async_copy(part, part, recv_sem.at[stage]).wait()

    def departed(stage, over_seq, target):
        part = target.at[pl.ds(0, (n_seq if over_seq else n_ten) - 1)]
        pltpu.make_async_copy(part, part, send_sem.at[stage]).wait()

    def normalise(blocks, gain, bias):
        total = jnp.zeros((rows_own, 1), F32)
        square = jnp.zeros((rows_own, 1), F32)
        for c in range(n_ten):
            part = blocks[c].astype(F32)
            total += jnp.sum(part, -1, keepdims=True)
            square += jnp.sum(part * part, -1, keepdims=True)
        average = total / width
        inverse = lax.rsqrt(square / width - average * average + EPSILON)
        for c in range(n_ten):
            at = slice(c * cols, (c + 1) * cols)
            part = blocks[c].astype(F32)
            nrm[:, at] = ((part - average) * inverse * gain[:, at] + bias[:, at]).astype(BF16)

    steps, requests = tok_ref.shape
    own_requests = rows_own // steps
    small = jnp.concatenate(
        [
            tok_ref[...].astype(F32),
            jnp.broadcast_to(len_ref[...].astype(F32), (8 - steps, requests)),
        ],
        0,
    ).T
    upper = jnp.floor(small * (1.0 / 256.0))
    lower = (small - upper * 256.0).astype(BF16)
    upper = upper.astype(BF16)

    def expanded(selector):
        selector = jnp.where(selector, 1.0, 0.0).astype(BF16)
        return dot(selector, upper) * 256.0 + dot(selector, lower)

    by_row = expanded(iota((rows_all, requests), 0) // steps == iota((rows_all, requests), 1))
    step_lane = iota((rows_all, 8), 1) == iota((rows_all, 8), 0) % steps
    token = jnp.sum(jnp.where(step_lane, by_row, 0.0), -1, keepdims=True).astype(jnp.int32)
    token = token - me * emb.shape[0]

    loads[0].wait()
    vocab = emb.shape[0]
    tile_rows = min(rows_all, 128)
    for tile in range(rows_all // tile_rows):
        at = slice(tile * tile_rows, (tile + 1) * tile_rows)
        hit = token[at] == iota((tile_rows, vocab), 1)
        looked = dot(jnp.where(hit, 1.0, 0.0).astype(BF16), emb[...])
        blocks = tile_rows // rows_own
        send_a[tile * blocks : (tile + 1) * blocks] = looked.astype(BF16).reshape(
            blocks, rows_own, cols
        )

    home_shape = (rows_own, requests)
    home = expanded(me * own_requests + iota(home_shape, 0) // steps == iota(home_shape, 1))
    lane = iota((rows_own, cols), 1)
    feature = lane % HD
    position = home[:, steps : steps + 1] + (iota((rows_own, cols), 0) % steps).astype(F32)
    half_rot = ROT // 2
    frequency = jnp.zeros((rows_own, cols), F32)
    for i in range(half_rot):
        frequency = jnp.where(feature % half_rot == i, THETA ** (-2.0 * i / ROT), frequency)
    angle = position * frequency
    turns = jnp.floor(angle * 0.6366197723675814 + 0.5)
    quadrant = turns.astype(jnp.int32) % 4
    arc = angle - turns * 1.5703125
    arc = arc - turns * 4.837512969970703125e-4
    arc = arc - turns * 7.54978995489188216e-8
    arc2 = arc * arc
    sin_arc = ((-1.9515295891e-4 * arc2 + 8.3321608736e-3) * arc2 - 1.6666654611e-1) * arc2
    sin_arc = sin_arc * arc + arc
    cos_arc = (2.443315711809948e-5 * arc2 - 1.388731625493765e-3) * arc2
    cos_arc = (cos_arc + 4.166664568298827e-2) * arc2 * arc2 - 0.5 * arc2 + 1.0
    odd = quadrant % 2 == 1
    sine = jnp.where(odd, cos_arc, sin_arc)
    sine = jnp.where(quadrant >= 2, -sine, sine)
    cosine = jnp.where(odd, sin_arc, cos_arc)
    cosine = jnp.where((quadrant == 1) | (quadrant == 2), -cosine, cosine)
    first_half = feature < half_rot
    cos_wide = jnp.where(feature < ROT, cosine, 1.0)
    sin_wide = jnp.where(feature < ROT, jnp.where(first_half, -sine, sine), 0.0)

    most = table_ref.shape[0]
    table = table_ref[...].astype(F32).T.astype(jnp.int32)
    grid = (requests, 128)
    slot_id = me * slots + iota(grid, 1)
    request_id = iota(grid, 0)
    length = jnp.broadcast_to(small[:, steps : steps + 1].astype(jnp.int32), grid)
    owner = jnp.zeros(grid, jnp.int32)
    filled = jnp.zeros(grid, jnp.int32)
    leads = jnp.zeros(grid, jnp.int32)
    for j in range(most):
        match = table[:, j : j + 1] == slot_id
        owner = jnp.where(match, request_id, owner)
        filled = jnp.where(match, jnp.clip(length - j * page, 0, page), filled)
        if j == 0:
            leads = jnp.where(match, request_id + 1, leads)
    owner = jnp.sum(owner.astype(F32), 0, keepdims=True).astype(jnp.int32) * steps
    filled = jnp.sum(filled.astype(F32), 0, keepdims=True).astype(jnp.int32)
    leads = jnp.sum(leads.astype(F32), 0, keepdims=True)
    spot = iota((1, page), 1)
    for s in range(slots):
        posown[:, s * page : (s + 1) * page] = jnp.where(
            spot < filled[:, s : s + 1], owner[:, s : s + 1], -8
        )
    rows_slot = slots * steps * heads
    leads = jnp.broadcast_to(leads, (8, 128)).astype(BF16)
    per_slot = steps * heads
    slot_of = (iota((rows_slot, 128), 0) // per_slot == iota((rows_slot, 128), 1)).astype(F32)
    leader = dot_nt(slot_of.astype(BF16), leads)[:, :1].astype(jnp.int32)
    row_step = (iota((rows_slot, 1), 0) // heads) % steps
    row_code = jnp.where(leader > 0, (leader - 1) * steps + row_step, -1)
    slot_of = (iota((128, rows_slot), 1) // per_slot == iota((128, rows_slot), 0)).astype(F32)
    leader = dot(leads, slot_of.astype(BF16))[:1].astype(jnp.int32)
    lane_step = (iota((1, rows_slot), 1) // heads) % steps
    lane_code = jnp.where(leader > 0, (leader - 1) * steps + lane_step, -1)
    pick[...] = jnp.where(row_code == iota((rows_slot, rows_all), 1), 1.0, 0.0).astype(BF16)
    put[...] = jnp.where(lane_code == iota((rows_all, rows_slot), 0), 1.0, 0.0).astype(BF16)
    wanted = iota((rows_all, 1), 0)
    wanted = wanted % requests * steps + wanted // requests
    turn[...] = jnp.where(wanted == iota((rows_all, rows_all), 1), 1.0, 0.0).astype(BF16)

    pl.semaphore_wait(barrier, n_seq + n_ten - 2)
    all_to_all(0, True, send_a, recv_a)
    own_part = send_a[me].astype(F32)
    arrived(0, True, recv_a)
    residual = own_part + jnp.sum(recv_a[...].astype(F32), 0)
    res_own[...] = residual.astype(BF16)
    spread(1, False, res_own, res_all)
    res_all[mt] = residual.astype(BF16)
    arrived(1, False, res_all)
    normalise(res_all, g1_ref, b1_ref)

    def rotated(field):
        partner = jnp.where(
            first_half,
            pltpu.roll(field, cols - ROT // 2, 1),
            pltpu.roll(field, ROT // 2, 1),
        )
        return field * cos_wide + partner * sin_wide

    loads[1].wait()
    queries = rotated(dot(nrm[...], wq[...]) + qb_ref[...]).astype(BF16)
    q_own[...] = queries
    spread(2, True, q_own, q_all)
    q_all[me] = queries
    loads[2].wait()
    loads[3].wait()
    new_keys = rotated(dot(nrm[...], wk[...]) + kb_ref[...]).astype(BF16)
    new_values = (dot(nrm[...], wv[...]) + vb_ref[...]).astype(BF16)

    scale = HD**-0.5
    head_of = lane // HD
    q_tall = jnp.concatenate(
        [jnp.where(head_of == h, queries, jnp.zeros_like(queries)) for h in range(heads)], 0
    )
    tall = (heads * rows_own, rows_own)
    query_row = iota(tall, 0) % rows_own
    key_row = iota(tall, 1)
    seen = (query_row // steps == key_row // steps) & (key_row <= query_row)
    fresh = jnp.where(seen, dot_nt(q_tall, new_keys) * scale, NEGATIVE)
    fresh_top = jnp.max(fresh, -1, keepdims=True)
    fresh_weights = jnp.where(seen, jnp.exp(fresh - fresh_top), 0.0).astype(BF16)
    fresh_mass = jnp.sum(fresh_weights.astype(F32), -1, keepdims=True)
    fresh_mix = dot(fresh_weights, new_values)
    top_wide = jnp.zeros((rows_own, cols), F32)
    mass_wide = jnp.zeros((rows_own, cols), F32)
    mix_wide = jnp.zeros((rows_own, cols), F32)
    for h in range(heads):
        at = slice(h * rows_own, (h + 1) * rows_own)
        top_wide = jnp.where(head_of == h, fresh_top[at], top_wide)
        mass_wide = jnp.where(head_of == h, fresh_mass[at], mass_wide)
        mix_wide = jnp.where(head_of == h, fresh_mix[at], mix_wide)

    arrived(2, True, q_all)
    picked = dot(pick[...], q_all[...].reshape(rows_all, cols))
    row_head = iota((rows_slot, cols), 0) % heads
    own_head = row_head == iota((rows_slot, cols), 1) // HD
    q_rows[...] = jnp.where(own_head, picked, 0.0).astype(BF16)
    row_owner = row_code - row_step
    group = 4 if slots % 4 == 0 else 1
    span = group * page
    loads[4].wait()
    top = jnp.full((rows_slot, 1), NEGATIVE, F32)
    for g in range(slots // group):
        at = slice(g * span, (g + 1) * span)
        keys = kc[g * group : (g + 1) * group].reshape(span, cols)
        scores = dot_nt(q_rows[...], keys) * scale
        scores = jnp.where(row_owner == posown[:, at], scores, NEGATIVE)
        sbuf[:, at] = scores
        top = jnp.maximum(top, jnp.max(scores, -1, keepdims=True))
    loads[5].wait()
    mass = jnp.zeros((rows_slot, 1), F32)
    mix = jnp.zeros((rows_slot, cols), F32)
    for g in range(slots // group):
        at = slice(g * span, (g + 1) * span)
        weights = jnp.exp(sbuf[:, at] - top).astype(BF16)
        mass += jnp.sum(weights.astype(F32), -1, keepdims=True)
        mix += dot(weights, vc[g * group : (g + 1) * group].reshape(span, cols))
    level = top + jnp.log(mass)
    high = level.astype(BF16).astype(F32)
    middle = (level - high).astype(BF16).astype(F32)
    low = level - high - middle
    xbuf[:, :cols] = jnp.where(own_head, mix / mass, 0.0).astype(BF16)
    extra = xbuf.shape[1] - cols
    place = iota((rows_slot, extra), 1)
    head_col = iota((rows_slot, extra), 0) % heads
    parts = jnp.where(place == head_col, high, 0.0)
    parts = jnp.where(place == head_col + heads, middle, parts)
    parts = jnp.where(place == head_col + 2 * heads, low, parts)
    xbuf[:, cols:] = parts.astype(BF16)
    send_c[...] = dot(put[...], xbuf[...]).astype(BF16).reshape(n_seq, rows_own, cols + extra)
    all_to_all(3, True, send_c, recv_c)
    own_part = send_c[me].astype(F32)
    arrived(3, True, recv_c)
    returned = own_part + jnp.sum(recv_c[...].astype(F32), 0)
    lift = iota((extra, cols), 0)
    lift = jnp.where(
        (lift < 3 * heads) & (lift % heads == iota((extra, cols), 1) // HD), 1.0, 0.0
    ).astype(BF16)
    page_level = dot(returned[:, cols:].astype(BF16), lift)
    overall = jnp.maximum(page_level, top_wide)
    page_factor = jnp.exp(page_level - overall)
    fresh_factor = jnp.exp(top_wide - overall)
    attended = (returned[:, :cols] * page_factor + mix_wide * fresh_factor) / (
        page_factor + mass_wide * fresh_factor
    )

    loads[6].wait()
    partial = dot(attended.astype(BF16), wo[...]).astype(BF16)
    for c in range(n_ten):
        send_e[c] = partial[:, c * cols : (c + 1) * cols]
    all_to_all(4, False, send_e, recv_e)
    own_part = send_e[mt].astype(F32)
    arrived(4, False, recv_e)
    attn_total = own_part + jnp.sum(recv_e[...].astype(F32), 0)
    hidden_one = (residual + attn_total).astype(BF16)
    h1_own[...] = hidden_one
    spread(5, False, h1_own, h1_all)
    h1_all[mt] = hidden_one
    arrived(5, False, h1_all)
    normalise(h1_all, g2_ref, b2_ref)
    loads[7].wait()
    loads[8].wait()
    gate = dot(nrm[...], wg[...])
    up = dot(nrm[...], wu[...])
    activated = (gate / (1.0 + jnp.exp(-gate)) * up).astype(BF16)
    loads[9].wait()
    partial = dot(activated, wd[...]).astype(BF16)
    for c in range(n_ten):
        send_h[c] = partial[:, c * cols : (c + 1) * cols]
    all_to_all(6, False, send_h, recv_h)
    own_part = send_h[mt].astype(F32)
    arrived(6, False, recv_h)
    mlp_total = own_part + jnp.sum(recv_h[...].astype(F32), 0)
    output = (hidden_one.astype(F32) + mlp_total).astype(BF16)
    out_own[...] = output
    spread(7, True, out_own, out_all)
    out_all[me] = output
    departed(0, True, recv_a)
    departed(1, False, res_all)
    departed(2, True, q_all)
    departed(3, True, recv_c)
    departed(4, False, recv_e)
    departed(5, False, h1_all)
    departed(6, False, recv_h)
    arrived(7, True, out_all)
    out_ref[...] = dot(turn[...], out_all[...].reshape(rows_all, cols)).astype(BF16)
    departed(7, True, out_all)


def shards(
    n_seq,
    n_ten,
    tokens,
    lengths,
    page_table,
    embedding,
    ln1_gain,
    ln1_bias,
    w_query,
    q_bias,
    w_key,
    k_bias,
    w_value,
    v_bias,
    w_out,
    ln2_gain,
    ln2_bias,
    w_gate,
    w_up,
    w_down,
    k_cache,
    v_cache,
):
    steps, requests = tokens.shape
    rows_all = steps * requests
    rows_own = rows_all // n_seq
    slots, page, cols = k_cache.shape
    heads = cols // HD
    width = n_ten * cols
    rows_slot = slots * steps * heads

    vmem = pl.BlockSpec(memory_space=pltpu.VMEM)
    hbm = pl.BlockSpec(memory_space=pl.ANY)
    extra = 128
    scratch = lambda *shape: pltpu.VMEM(shape, BF16)
    out = pl.pallas_call(
        functools.partial(layer_kernel, n_seq, n_ten),
        out_shape=jax.ShapeDtypeStruct((rows_all, cols), BF16),
        in_specs=[vmem] * 10 + [hbm] * 10,
        out_specs=vmem,
        scratch_shapes=[
            scratch(*embedding.shape),
            scratch(*w_query.shape),
            scratch(*w_key.shape),
            scratch(*w_value.shape),
            scratch(*w_out.shape),
            scratch(*w_gate.shape),
            scratch(*w_up.shape),
            scratch(*w_down.shape),
            scratch(*k_cache.shape),
            scratch(*v_cache.shape),
            scratch(n_seq, rows_own, cols),
            scratch(n_seq - 1, rows_own, cols),
            scratch(rows_own, cols),
            scratch(n_ten, rows_own, cols),
            scratch(rows_own, width),
            scratch(rows_own, cols),
            scratch(n_seq, rows_own, cols),
            scratch(rows_slot, cols),
            pltpu.VMEM((rows_slot, slots * page), F32),
            scratch(rows_slot, cols + extra),
            scratch(n_seq, rows_own, cols + extra),
            scratch(n_seq - 1, rows_own, cols + extra),
            scratch(n_ten, rows_own, cols),
            scratch(n_ten - 1, rows_own, cols),
            scratch(rows_own, cols),
            scratch(n_ten, rows_own, cols),
            scratch(n_ten, rows_own, cols),
            scratch(n_ten - 1, rows_own, cols),
            scratch(rows_own, cols),
            scratch(n_seq, rows_own, cols),
            pltpu.VMEM((1, slots * page), jnp.int32),
            scratch(rows_slot, rows_all),
            scratch(rows_all, rows_slot),
            scratch(rows_all, rows_all),
            pltpu.SemaphoreType.DMA((10,)),
            pltpu.SemaphoreType.DMA((8,)),
            pltpu.SemaphoreType.DMA((8,)),
        ],
        compiler_params=pltpu.CompilerParams(
            collective_id=0, has_side_effects=True, vmem_limit_bytes=62 * 1024 * 1024
        ),
        name="layer",
    )(
        tokens,
        lengths[None],
        page_table.T,
        ln1_gain[None],
        ln1_bias[None],
        q_bias[None],
        k_bias[None],
        v_bias[None],
        ln2_gain[None],
        ln2_bias[None],
        embedding,
        w_query,
        w_key,
        w_value,
        w_out,
        w_gate,
        w_up,
        w_down,
        k_cache,
        v_cache,
    )
    return out.reshape(steps, requests, cols)


def solution(mesh):
    placed = (
        P(),
        P(),
        P(),
        P("seq", "tensor"),
        P(),
        P(),
        P(None, "tensor"),
        P("tensor"),
        P(None, "tensor"),
        P("tensor"),
        P(None, "tensor"),
        P("tensor"),
        P("tensor", None),
        P(),
        P(),
        P(None, "tensor"),
        P(None, "tensor"),
        P("tensor", None),
        P("seq", None, "tensor"),
        P("seq", None, "tensor"),
    )
    return jax.shard_map(
        functools.partial(shards, mesh.shape["seq"], mesh.shape["tensor"]),
        mesh=mesh,
        in_specs=placed,
        out_specs=P(None, None, "tensor"),
        check_vma=False,
    )
```

```python
import functools

import jax
import jax.numpy as jnp
from jax import lax
from jax.experimental import pallas as pl
from jax.experimental.pallas import tpu as pltpu
from jax.sharding import PartitionSpec as P

HD = 64
ROT = 16
EPSILON = 1e-05
NEGATIVE = -1e30
THETA = 10000.0
MESH = pl.DeviceIdType.MESH
F32 = jnp.float32
BF16 = jnp.bfloat16


def iota(shape, axis):
    return lax.broadcasted_iota(jnp.int32, shape, axis)


def dot(left, right):
    return jnp.dot(left, right, preferred_element_type=F32)


def dot_nt(left, right):
    return lax.dot_general(left, right, (((1,), (1,)), ((), ())), preferred_element_type=F32)


def layer_kernel(
    n_seq,
    n_ten,
    tok_ref,
    len_ref,
    table_ref,
    g1_ref,
    b1_ref,
    qb_ref,
    kb_ref,
    vb_ref,
    g2_ref,
    b2_ref,
    emb_hbm,
    wq_hbm,
    wk_hbm,
    wv_hbm,
    wo_hbm,
    wg_hbm,
    wu_hbm,
    wd_hbm,
    kc_hbm,
    vc_hbm,
    out_ref,
    emb,
    wq,
    wk,
    wv,
    wo,
    wg,
    wu,
    wd,
    kc,
    vc,
    send_a,
    recv_a,
    res_own,
    res_all,
    nrm,
    q_own,
    q_all,
    q_rows,
    sbuf,
    xbuf,
    send_c,
    recv_c,
    send_e,
    recv_e,
    h1_own,
    h1_all,
    send_h,
    recv_h,
    out_own,
    out_all,
    posown,
    pick,
    put,
    turn,
    load_sem,
    send_sem,
    recv_sem,
):
    me = lax.axis_index("seq")
    mt = lax.axis_index("tensor")
    rows_own, cols = q_own.shape
    heads = cols // HD
    slots, page = kc.shape[0], kc.shape[1]
    rows_all = n_seq * rows_own
    width = n_ten * cols

    loads = []
    for index, (source, target) in enumerate(
        (
            (emb_hbm, emb),
            (wq_hbm, wq),
            (wk_hbm, wk),
            (wv_hbm, wv),
            (kc_hbm, kc),
            (vc_hbm, vc),
            (wo_hbm, wo),
            (wg_hbm, wg),
            (wu_hbm, wu),
            (wd_hbm, wd),
        )
    ):
        copy = pltpu.make_async_copy(source, target, load_sem.at[index])
        copy.start()
        loads.append(copy)

    barrier = pltpu.get_barrier_semaphore()

    @pl.loop(1, n_seq)
    def _(step):
        pl.semaphore_signal(
            barrier, inc=1, device_id=(lax.rem(me + step, n_seq), mt), device_id_type=MESH
        )

    @pl.loop(1, n_ten)
    def _(step):
        pl.semaphore_signal(
            barrier, inc=1, device_id=(me, lax.rem(mt + step, n_ten)), device_id_type=MESH
        )

    major, minor = (n_seq // 8, 8) if n_seq % 8 == 0 else (1, n_seq)

    def far(offset, size):
        return min(offset, size - offset)

    seq_offsets = [(i, j) for i in range(major) for j in range(minor) if i or j]
    seq_offsets.sort(
        key=lambda o: (
            -far(o[0], major) - far(o[1], minor),
            far(o[0], major),
            o[0] + o[1],
        )
    )
    ten_offsets = sorted(range(1, n_ten), key=lambda o: -far(o // 2, n_ten // 2))

    def partners(over_seq):
        if over_seq:
            for slot, (i, j) in enumerate(seq_offsets):
                peer = lax.rem(me // minor + i, major) * minor + lax.rem(me % minor + j, minor)
                yield slot, peer, (peer, mt)
        else:
            for slot, offset in enumerate(ten_offsets):
                chip = lax.rem(mt // 2 + offset // 2, n_ten // 2)
                peer = chip * 2 + lax.rem(mt % 2 + offset % 2, 2)
                yield slot, peer, (me, peer)

    def all_to_all(stage, over_seq, source, target):
        for slot, peer, device in partners(over_seq):
            pltpu.make_async_remote_copy(
                src_ref=source.at[peer],
                dst_ref=target.at[slot],
                send_sem=send_sem.at[stage],
                recv_sem=recv_sem.at[stage],
                device_id=device,
                device_id_type=MESH,
            ).start()

    def spread(stage, over_seq, source, target):
        own = me if over_seq else mt
        for slot, peer, device in partners(over_seq):
            pltpu.make_async_remote_copy(
                src_ref=source,
                dst_ref=target.at[own],
                send_sem=send_sem.at[stage],
                recv_sem=recv_sem.at[stage],
                device_id=device,
                device_id_type=MESH,
            ).start()

    def arrived(stage, over_seq, target):
        part = target.at[pl.ds(0, (n_seq if over_seq else n_ten) - 1)]
        pltpu.make_async_copy(part, part, recv_sem.at[stage]).wait()

    def departed(stage, over_seq, target):
        part = target.at[pl.ds(0, (n_seq if over_seq else n_ten) - 1)]
        pltpu.make_async_copy(part, part, send_sem.at[stage]).wait()

    def normalise(blocks, gain, bias):
        total = jnp.zeros((rows_own, 1), F32)
        square = jnp.zeros((rows_own, 1), F32)
        for c in range(n_ten):
            part = blocks[c].astype(F32)
            total += jnp.sum(part, -1, keepdims=True)
            square += jnp.sum(part * part, -1, keepdims=True)
        average = total / width
        inverse = lax.rsqrt(square / width - average * average + EPSILON)
        for c in range(n_ten):
            at = slice(c * cols, (c + 1) * cols)
            part = blocks[c].astype(F32)
            nrm[:, at] = ((part - average) * inverse * gain[:, at] + bias[:, at]).astype(BF16)

    steps, requests = tok_ref.shape
    own_requests = rows_own // steps
    small = jnp.concatenate(
        [
            tok_ref[...].astype(F32),
            jnp.broadcast_to(len_ref[...].astype(F32), (8 - steps, requests)),
        ],
        0,
    ).T
    upper = jnp.floor(small * (1.0 / 256.0))
    lower = (small - upper * 256.0).astype(BF16)
    upper = upper.astype(BF16)

    def expanded(selector):
        selector = jnp.where(selector, 1.0, 0.0).astype(BF16)
        return dot(selector, upper) * 256.0 + dot(selector, lower)

    by_row = expanded(iota((rows_all, requests), 0) // steps == iota((rows_all, requests), 1))
    step_lane = iota((rows_all, 8), 1) == iota((rows_all, 8), 0) % steps
    token = jnp.sum(jnp.where(step_lane, by_row, 0.0), -1, keepdims=True).astype(jnp.int32)
    token = token - me * emb.shape[0]

    loads[0].wait()
    vocab = emb.shape[0]
    tile_rows = min(rows_all, 128)
    for tile in range(rows_all // tile_rows):
        at = slice(tile * tile_rows, (tile + 1) * tile_rows)
        hit = token[at] == iota((tile_rows, vocab), 1)
        looked = dot(jnp.where(hit, 1.0, 0.0).astype(BF16), emb[...])
        blocks = tile_rows // rows_own
        send_a[tile * blocks : (tile + 1) * blocks] = looked.astype(BF16).reshape(
            blocks, rows_own, cols
        )

    home_shape = (rows_own, requests)
    home = expanded(me * own_requests + iota(home_shape, 0) // steps == iota(home_shape, 1))
    lane = iota((rows_own, cols), 1)
    feature = lane % HD
    position = home[:, steps : steps + 1] + (iota((rows_own, cols), 0) % steps).astype(F32)
    half_rot = ROT // 2
    frequency = jnp.zeros((rows_own, cols), F32)
    for i in range(half_rot):
        frequency = jnp.where(feature % half_rot == i, THETA ** (-2.0 * i / ROT), frequency)
    angle = position * frequency
    turns = jnp.floor(angle * 0.6366197723675814 + 0.5)
    quadrant = turns.astype(jnp.int32) % 4
    arc = angle - turns * 1.5703125
    arc = arc - turns * 4.837512969970703125e-4
    arc = arc - turns * 7.54978995489188216e-8
    arc2 = arc * arc
    sin_arc = ((-1.9515295891e-4 * arc2 + 8.3321608736e-3) * arc2 - 1.6666654611e-1) * arc2
    sin_arc = sin_arc * arc + arc
    cos_arc = (2.443315711809948e-5 * arc2 - 1.388731625493765e-3) * arc2
    cos_arc = (cos_arc + 4.166664568298827e-2) * arc2 * arc2 - 0.5 * arc2 + 1.0
    odd = quadrant % 2 == 1
    sine = jnp.where(odd, cos_arc, sin_arc)
    sine = jnp.where(quadrant >= 2, -sine, sine)
    cosine = jnp.where(odd, sin_arc, cos_arc)
    cosine = jnp.where((quadrant == 1) | (quadrant == 2), -cosine, cosine)
    first_half = feature < half_rot
    cos_wide = jnp.where(feature < ROT, cosine, 1.0)
    sin_wide = jnp.where(feature < ROT, jnp.where(first_half, -sine, sine), 0.0)

    most = table_ref.shape[0]
    table = table_ref[...].astype(F32).T.astype(jnp.int32)
    grid = (requests, 128)
    slot_id = me * slots + iota(grid, 1)
    request_id = iota(grid, 0)
    length = jnp.broadcast_to(small[:, steps : steps + 1].astype(jnp.int32), grid)
    owner = jnp.zeros(grid, jnp.int32)
    filled = jnp.zeros(grid, jnp.int32)
    leads = jnp.zeros(grid, jnp.int32)
    for j in range(most):
        match = table[:, j : j + 1] == slot_id
        owner = jnp.where(match, request_id, owner)
        filled = jnp.where(match, jnp.clip(length - j * page, 0, page), filled)
        if j == 0:
            leads = jnp.where(match, request_id + 1, leads)
    owner = jnp.sum(owner.astype(F32), 0, keepdims=True).astype(jnp.int32) * steps
    filled = jnp.sum(filled.astype(F32), 0, keepdims=True).astype(jnp.int32)
    leads = jnp.sum(leads.astype(F32), 0, keepdims=True)
    spot = iota((1, page), 1)
    for s in range(slots):
        posown[:, s * page : (s + 1) * page] = jnp.where(
            spot < filled[:, s : s + 1], owner[:, s : s + 1], -8
        )
    rows_slot = slots * steps * heads
    leads = jnp.broadcast_to(leads, (8, 128)).astype(BF16)
    per_slot = steps * heads
    slot_of = (iota((rows_slot, 128), 0) // per_slot == iota((rows_slot, 128), 1)).astype(F32)
    leader = dot_nt(slot_of.astype(BF16), leads)[:, :1].astype(jnp.int32)
    row_step = (iota((rows_slot, 1), 0) // heads) % steps
    row_code = jnp.where(leader > 0, (leader - 1) * steps + row_step, -1)
    slot_of = (iota((128, rows_slot), 1) // per_slot == iota((128, rows_slot), 0)).astype(F32)
    leader = dot(leads, slot_of.astype(BF16))[:1].astype(jnp.int32)
    lane_step = (iota((1, rows_slot), 1) // heads) % steps
    lane_code = jnp.where(leader > 0, (leader - 1) * steps + lane_step, -1)
    pick[...] = jnp.where(row_code == iota((rows_slot, rows_all), 1), 1.0, 0.0).astype(BF16)
    put[...] = jnp.where(lane_code == iota((rows_all, rows_slot), 0), 1.0, 0.0).astype(BF16)
    wanted = iota((rows_all, 1), 0)
    wanted = wanted % requests * steps + wanted // requests
    turn[...] = jnp.where(wanted == iota((rows_all, rows_all), 1), 1.0, 0.0).astype(BF16)

    pl.semaphore_wait(barrier, n_seq + n_ten - 2)
    all_to_all(0, True, send_a, recv_a)
    own_part = send_a[me].astype(F32)
    arrived(0, True, recv_a)
    residual = own_part + jnp.sum(recv_a[...].astype(F32), 0)
    res_own[...] = residual.astype(BF16)
    spread(1, False, res_own, res_all)
    res_all[mt] = residual.astype(BF16)
    arrived(1, False, res_all)
    normalise(res_all, g1_ref, b1_ref)

    def rotated(field):
        partner = jnp.where(
            first_half,
            pltpu.roll(field, cols - ROT // 2, 1),
            pltpu.roll(field, ROT // 2, 1),
        )
        return field * cos_wide + partner * sin_wide

    loads[1].wait()
    queries = rotated(dot(nrm[...], wq[...]) + qb_ref[...]).astype(BF16)
    q_own[...] = queries
    spread(2, True, q_own, q_all)
    q_all[me] = queries
    loads[2].wait()
    loads[3].wait()
    new_keys = rotated(dot(nrm[...], wk[...]) + kb_ref[...]).astype(BF16)
    new_values = (dot(nrm[...], wv[...]) + vb_ref[...]).astype(BF16)

    scale = HD**-0.5
    head_of = lane // HD
    q_tall = jnp.concatenate(
        [jnp.where(head_of == h, queries, jnp.zeros_like(queries)) for h in range(heads)], 0
    )
    tall = (heads * rows_own, rows_own)
    query_row = iota(tall, 0) % rows_own
    key_row = iota(tall, 1)
    seen = (query_row // steps == key_row // steps) & (key_row <= query_row)
    fresh = jnp.where(seen, dot_nt(q_tall, new_keys) * scale, NEGATIVE)
    fresh_top = jnp.max(fresh, -1, keepdims=True)
    fresh_weights = jnp.where(seen, jnp.exp(fresh - fresh_top), 0.0).astype(BF16)
    fresh_mass = jnp.sum(fresh_weights.astype(F32), -1, keepdims=True)
    fresh_mix = dot(fresh_weights, new_values)
    top_wide = jnp.zeros((rows_own, cols), F32)
    mass_wide = jnp.zeros((rows_own, cols), F32)
    mix_wide = jnp.zeros((rows_own, cols), F32)
    for h in range(heads):
        at = slice(h * rows_own, (h + 1) * rows_own)
        top_wide = jnp.where(head_of == h, fresh_top[at], top_wide)
        mass_wide = jnp.where(head_of == h, fresh_mass[at], mass_wide)
        mix_wide = jnp.where(head_of == h, fresh_mix[at], mix_wide)

    arrived(2, True, q_all)
    picked = dot(pick[...], q_all[...].reshape(rows_all, cols))
    row_head = iota((rows_slot, cols), 0) % heads
    own_head = row_head == iota((rows_slot, cols), 1) // HD
    q_rows[...] = jnp.where(own_head, picked, 0.0).astype(BF16)
    row_owner = row_code - row_step
    group = 4 if slots % 4 == 0 else 1
    span = group * page
    loads[4].wait()
    top = jnp.full((rows_slot, 1), NEGATIVE, F32)
    for g in range(slots // group):
        at = slice(g * span, (g + 1) * span)
        keys = kc[g * group : (g + 1) * group].reshape(span, cols)
        scores = dot_nt(q_rows[...], keys) * scale
        scores = jnp.where(row_owner == posown[:, at], scores, NEGATIVE)
        sbuf[:, at] = scores
        top = jnp.maximum(top, jnp.max(scores, -1, keepdims=True))
    loads[5].wait()
    mass = jnp.zeros((rows_slot, 1), F32)
    mix = jnp.zeros((rows_slot, cols), F32)
    for g in range(slots // group):
        at = slice(g * span, (g + 1) * span)
        weights = jnp.exp(sbuf[:, at] - top).astype(BF16)
        mass += jnp.sum(weights.astype(F32), -1, keepdims=True)
        mix += dot(weights, vc[g * group : (g + 1) * group].reshape(span, cols))
    level = top + jnp.log(mass)
    high = level.astype(BF16).astype(F32)
    middle = (level - high).astype(BF16).astype(F32)
    low = level - high - middle
    xbuf[:, :cols] = jnp.where(own_head, mix / mass, 0.0).astype(BF16)
    extra = xbuf.shape[1] - cols
    place = iota((rows_slot, extra), 1)
    head_col = iota((rows_slot, extra), 0) % heads
    parts = jnp.where(place == head_col, high, 0.0)
    parts = jnp.where(place == head_col + heads, middle, parts)
    parts = jnp.where(place == head_col + 2 * heads, low, parts)
    xbuf[:, cols:] = parts.astype(BF16)
    send_c[...] = dot(put[...], xbuf[...]).astype(BF16).reshape(n_seq, rows_own, cols + extra)
    all_to_all(3, True, send_c, recv_c)
    own_part = send_c[me].astype(F32)
    arrived(3, True, recv_c)
    returned = own_part + jnp.sum(recv_c[...].astype(F32), 0)
    lift = iota((extra, cols), 0)
    lift = jnp.where(
        (lift < 3 * heads) & (lift % heads == iota((extra, cols), 1) // HD), 1.0, 0.0
    ).astype(BF16)
    page_level = dot(returned[:, cols:].astype(BF16), lift)
    overall = jnp.maximum(page_level, top_wide)
    page_factor = jnp.exp(page_level - overall)
    fresh_factor = jnp.exp(top_wide - overall)
    attended = (returned[:, :cols] * page_factor + mix_wide * fresh_factor) / (
        page_factor + mass_wide * fresh_factor
    )

    loads[6].wait()
    partial = dot(attended.astype(BF16), wo[...]).astype(BF16)
    for c in range(n_ten):
        send_e[c] = partial[:, c * cols : (c + 1) * cols]
    all_to_all(4, False, send_e, recv_e)
    own_part = send_e[mt].astype(F32)
    arrived(4, False, recv_e)
    attn_total = own_part + jnp.sum(recv_e[...].astype(F32), 0)
    hidden_one = (residual + attn_total).astype(BF16)
    h1_own[...] = hidden_one
    spread(5, False, h1_own, h1_all)
    h1_all[mt] = hidden_one
    arrived(5, False, h1_all)
    normalise(h1_all, g2_ref, b2_ref)
    loads[7].wait()
    loads[8].wait()
    gate = dot(nrm[...], wg[...])
    up = dot(nrm[...], wu[...])
    activated = (gate / (1.0 + jnp.exp(-gate)) * up).astype(BF16)
    loads[9].wait()
    partial = dot(activated, wd[...]).astype(BF16)
    for c in range(n_ten):
        send_h[c] = partial[:, c * cols : (c + 1) * cols]
    all_to_all(6, False, send_h, recv_h)
    own_part = send_h[mt].astype(F32)
    arrived(6, False, recv_h)
    mlp_total = own_part + jnp.sum(recv_h[...].astype(F32), 0)
    output = (hidden_one.astype(F32) + mlp_total).astype(BF16)
    out_own[...] = output
    spread(7, True, out_own, out_all)
    out_all[me] = output
    departed(0, True, recv_a)
    departed(1, False, res_all)
    departed(2, True, q_all)
    departed(3, True, recv_c)
    departed(4, False, recv_e)
    departed(5, False, h1_all)
    departed(6, False, recv_h)
    arrived(7, True, out_all)
    out_ref[...] = dot(turn[...], out_all[...].reshape(rows_all, cols)).astype(BF16)
    departed(7, True, out_all)


def shards(
    n_seq,
    n_ten,
    tokens,
    lengths,
    page_table,
    embedding,
    ln1_gain,
    ln1_bias,
    w_query,
    q_bias,
    w_key,
    k_bias,
    w_value,
    v_bias,
    w_out,
    ln2_gain,
    ln2_bias,
    w_gate,
    w_up,
    w_down,
    k_cache,
    v_cache,
):
    steps, requests = tokens.shape
    rows_all = steps * requests
    rows_own = rows_all // n_seq
    slots, page, cols = k_cache.shape
    heads = cols // HD
    width = n_ten * cols
    rows_slot = slots * steps * heads

    vmem = pl.BlockSpec(memory_space=pltpu.VMEM)
    hbm = pl.BlockSpec(memory_space=pl.ANY)
    extra = 128
    scratch = lambda *shape: pltpu.VMEM(shape, BF16)
    out = pl.pallas_call(
        functools.partial(layer_kernel, n_seq, n_ten),
        out_shape=jax.ShapeDtypeStruct((rows_all, cols), BF16),
        in_specs=[vmem] * 10 + [hbm] * 10,
        out_specs=vmem,
        scratch_shapes=[
            scratch(*embedding.shape),
            scratch(*w_query.shape),
            scratch(*w_key.shape),
            scratch(*w_value.shape),
            scratch(*w_out.shape),
            scratch(*w_gate.shape),
            scratch(*w_up.shape),
            scratch(*w_down.shape),
            scratch(*k_cache.shape),
            scratch(*v_cache.shape),
            scratch(n_seq, rows_own, cols),
            scratch(n_seq - 1, rows_own, cols),
            scratch(rows_own, cols),
            scratch(n_ten, rows_own, cols),
            scratch(rows_own, width),
            scratch(rows_own, cols),
            scratch(n_seq, rows_own, cols),
            scratch(rows_slot, cols),
            pltpu.VMEM((rows_slot, slots * page), F32),
            scratch(rows_slot, cols + extra),
            scratch(n_seq, rows_own, cols + extra),
            scratch(n_seq - 1, rows_own, cols + extra),
            scratch(n_ten, rows_own, cols),
            scratch(n_ten - 1, rows_own, cols),
            scratch(rows_own, cols),
            scratch(n_ten, rows_own, cols),
            scratch(n_ten, rows_own, cols),
            scratch(n_ten - 1, rows_own, cols),
            scratch(rows_own, cols),
            scratch(n_seq, rows_own, cols),
            pltpu.VMEM((1, slots * page), jnp.int32),
            scratch(rows_slot, rows_all),
            scratch(rows_all, rows_slot),
            scratch(rows_all, rows_all),
            pltpu.SemaphoreType.DMA((10,)),
            pltpu.SemaphoreType.DMA((8,)),
            pltpu.SemaphoreType.DMA((8,)),
        ],
        compiler_params=pltpu.CompilerParams(
            collective_id=0, has_side_effects=True, vmem_limit_bytes=62 * 1024 * 1024
        ),
        name="layer",
    )(
        tokens,
        lengths[None],
        page_table.T,
        ln1_gain[None],
        ln1_bias[None],
        q_bias[None],
        k_bias[None],
        v_bias[None],
        ln2_gain[None],
        ln2_bias[None],
        embedding,
        w_query,
        w_key,
        w_value,
        w_out,
        w_gate,
        w_up,
        w_down,
        k_cache,
        v_cache,
    )
    return out.reshape(steps, requests, cols)


def solution(mesh):
    placed = (
        P(),
        P(),
        P(),
        P("seq", "tensor"),
        P(),
        P(),
        P(None, "tensor"),
        P("tensor"),
        P(None, "tensor"),
        P("tensor"),
        P(None, "tensor"),
        P("tensor"),
        P("tensor", None),
        P(),
        P(),
        P(None, "tensor"),
        P(None, "tensor"),
        P("tensor", None),
        P("seq", None, "tensor"),
        P("seq", None, "tensor"),
    )
    return jax.shard_map(
        functools.partial(shards, mesh.shape["seq"], mesh.shape["tensor"]),
        mesh=mesh,
        in_specs=placed,
        out_specs=P(None, None, "tensor"),
        check_vma=False,
    )
```

```python
import functools

import jax
import jax.numpy as jnp
from jax import lax
from jax.experimental import pallas as pl
from jax.experimental.pallas import tpu as pltpu
from jax.sharding import PartitionSpec as P

HD = 64
ROT = 16
EPSILON = 1e-05
NEGATIVE = -1e30
THETA = 10000.0
MESH = pl.DeviceIdType.MESH
F32 = jnp.float32
BF16 = jnp.bfloat16


def iota(shape, axis):
    return lax.broadcasted_iota(jnp.int32, shape, axis)


def dot(left, right):
    return jnp.dot(left, right, preferred_element_type=F32)


def dot_nt(left, right):
    return lax.dot_general(left, right, (((1,), (1,)), ((), ())), preferred_element_type=F32)


def layer_kernel(
    n_seq,
    n_ten,
    tok_ref,
    len_ref,
    table_ref,
    g1_ref,
    b1_ref,
    qb_ref,
    kb_ref,
    vb_ref,
    g2_ref,
    b2_ref,
    emb_hbm,
    wq_hbm,
    wk_hbm,
    wv_hbm,
    wo_hbm,
    wg_hbm,
    wu_hbm,
    wd_hbm,
    kc_hbm,
    vc_hbm,
    out_ref,
    emb,
    wq,
    wk,
    wv,
    wo,
    wg,
    wu,
    wd,
    kc,
    vc,
    send_a,
    recv_a,
    res_own,
    res_all,
    nrm,
    q_own,
    q_all,
    q_rows,
    sbuf,
    xbuf,
    send_c,
    recv_c,
    send_l,
    recv_l,
    send_e,
    recv_e,
    h1_own,
    h1_all,
    send_h,
    recv_h,
    out_own,
    out_all,
    posown,
    pick,
    put,
    home_put,
    turn,
    load_sem,
    send_sem,
    recv_sem,
):
    me = lax.axis_index("seq")
    mt = lax.axis_index("tensor")
    rows_own, cols = q_own.shape
    heads = cols // HD
    slots, page = kc.shape[0], kc.shape[1]
    rows_all = n_seq * rows_own
    width = n_ten * cols

    loads = []
    for index, (source, target) in enumerate(
        (
            (emb_hbm, emb),
            (wq_hbm, wq),
            (wk_hbm, wk),
            (wv_hbm, wv),
            (kc_hbm, kc),
            (vc_hbm, vc),
            (wo_hbm, wo),
            (wg_hbm, wg),
            (wu_hbm, wu),
            (wd_hbm, wd),
        )
    ):
        copy = pltpu.make_async_copy(source, target, load_sem.at[index])
        copy.start()
        loads.append(copy)

    barrier = pltpu.get_barrier_semaphore()

    @pl.loop(1, n_seq)
    def _(step):
        pl.semaphore_signal(
            barrier, inc=1, device_id=(lax.rem(me + step, n_seq), mt), device_id_type=MESH
        )

    @pl.loop(1, n_ten)
    def _(step):
        pl.semaphore_signal(
            barrier, inc=1, device_id=(me, lax.rem(mt + step, n_ten)), device_id_type=MESH
        )

    major, minor = (n_seq // 8, 8) if n_seq % 8 == 0 else (1, n_seq)

    def far(offset, size):
        return min(offset, size - offset)

    seq_offsets = [(i, j) for i in range(major) for j in range(minor) if i or j]
    seq_offsets.sort(
        key=lambda o: (
            -far(o[0], major) - far(o[1], minor),
            far(o[0], major),
            o[0] + o[1],
        )
    )
    ten_offsets = sorted(range(1, n_ten), key=lambda o: -far(o // 2, n_ten // 2))

    def partners(over_seq):
        if over_seq:
            for slot, (i, j) in enumerate(seq_offsets):
                peer = lax.rem(me // minor + i, major) * minor + lax.rem(me % minor + j, minor)
                yield slot, peer, (peer, mt)
        else:
            for slot, offset in enumerate(ten_offsets):
                chip = lax.rem(mt // 2 + offset // 2, n_ten // 2)
                peer = chip * 2 + lax.rem(mt % 2 + offset % 2, 2)
                yield slot, peer, (me, peer)

    def all_to_all(stage, over_seq, source, target):
        for slot, peer, device in partners(over_seq):
            pltpu.make_async_remote_copy(
                src_ref=source.at[peer],
                dst_ref=target.at[slot],
                send_sem=send_sem.at[stage],
                recv_sem=recv_sem.at[stage],
                device_id=device,
                device_id_type=MESH,
            ).start()

    def spread(stage, over_seq, source, target):
        own = me if over_seq else mt
        for slot, peer, device in partners(over_seq):
            pltpu.make_async_remote_copy(
                src_ref=source,
                dst_ref=target.at[own],
                send_sem=send_sem.at[stage],
                recv_sem=recv_sem.at[stage],
                device_id=device,
                device_id_type=MESH,
            ).start()

    def arrived(stage, over_seq, target):
        part = target.at[pl.ds(0, (n_seq if over_seq else n_ten) - 1)]
        pltpu.make_async_copy(part, part, recv_sem.at[stage]).wait()

    def departed(stage, over_seq, target):
        part = target.at[pl.ds(0, (n_seq if over_seq else n_ten) - 1)]
        pltpu.make_async_copy(part, part, send_sem.at[stage]).wait()

    def normalise(blocks, gain, bias):
        total = jnp.zeros((rows_own, 1), F32)
        square = jnp.zeros((rows_own, 1), F32)
        for c in range(n_ten):
            part = blocks[c].astype(F32)
            total += jnp.sum(part, -1, keepdims=True)
            square += jnp.sum(part * part, -1, keepdims=True)
        average = total / width
        inverse = lax.rsqrt(square / width - average * average + EPSILON)
        for c in range(n_ten):
            at = slice(c * cols, (c + 1) * cols)
            part = blocks[c].astype(F32)
            nrm[:, at] = ((part - average) * inverse * gain[:, at] + bias[:, at]).astype(BF16)

    steps, requests = tok_ref.shape
    own_requests = rows_own // steps
    small = jnp.concatenate(
        [
            tok_ref[...].astype(F32),
            jnp.broadcast_to(len_ref[...].astype(F32), (8 - steps, requests)),
        ],
        0,
    ).T
    upper = jnp.floor(small * (1.0 / 256.0))
    lower = (small - upper * 256.0).astype(BF16)
    upper = upper.astype(BF16)

    def expanded(selector):
        selector = jnp.where(selector, 1.0, 0.0).astype(BF16)
        return dot(selector, upper) * 256.0 + dot(selector, lower)

    by_row = expanded(iota((rows_all, requests), 0) // steps == iota((rows_all, requests), 1))
    step_lane = iota((rows_all, 8), 1) == iota((rows_all, 8), 0) % steps
    token = jnp.sum(jnp.where(step_lane, by_row, 0.0), -1, keepdims=True).astype(jnp.int32)
    token = token - me * emb.shape[0]

    loads[0].wait()
    vocab = emb.shape[0]
    tile_rows = min(rows_all, 128)
    for tile in range(rows_all // tile_rows):
        at = slice(tile * tile_rows, (tile + 1) * tile_rows)
        hit = token[at] == iota((tile_rows, vocab), 1)
        looked = dot(jnp.where(hit, 1.0, 0.0).astype(BF16), emb[...])
        blocks = tile_rows // rows_own
        send_a[tile * blocks : (tile + 1) * blocks] = looked.astype(BF16).reshape(
            blocks, rows_own, cols
        )

    home_shape = (rows_own, requests)
    home = expanded(me * own_requests + iota(home_shape, 0) // steps == iota(home_shape, 1))
    lane = iota((rows_own, cols), 1)
    feature = lane % HD
    position = home[:, steps : steps + 1] + (iota((rows_own, cols), 0) % steps).astype(F32)
    half_rot = ROT // 2
    frequency = jnp.zeros((rows_own, cols), F32)
    for i in range(half_rot):
        frequency = jnp.where(feature % half_rot == i, THETA ** (-2.0 * i / ROT), frequency)
    angle = position * frequency
    turns = jnp.floor(angle * 0.6366197723675814 + 0.5)
    quadrant = turns.astype(jnp.int32) % 4
    arc = angle - turns * 1.5703125
    arc = arc - turns * 4.837512969970703125e-4
    arc = arc - turns * 7.54978995489188216e-8
    arc2 = arc * arc
    sin_arc = ((-1.9515295891e-4 * arc2 + 8.3321608736e-3) * arc2 - 1.6666654611e-1) * arc2
    sin_arc = sin_arc * arc + arc
    cos_arc = (2.443315711809948e-5 * arc2 - 1.388731625493765e-3) * arc2
    cos_arc = (cos_arc + 4.166664568298827e-2) * arc2 * arc2 - 0.5 * arc2 + 1.0
    odd = quadrant % 2 == 1
    sine = jnp.where(odd, cos_arc, sin_arc)
    sine = jnp.where(quadrant >= 2, -sine, sine)
    cosine = jnp.where(odd, sin_arc, cos_arc)
    cosine = jnp.where((quadrant == 1) | (quadrant == 2), -cosine, cosine)
    first_half = feature < half_rot
    cos_wide = jnp.where(feature < ROT, cosine, 1.0)
    sin_wide = jnp.where(feature < ROT, jnp.where(first_half, -sine, sine), 0.0)

    most = table_ref.shape[0]
    table = table_ref[...].astype(F32).T.astype(jnp.int32)
    grid = (requests, 128)
    slot_id = me * slots + iota(grid, 1)
    request_id = iota(grid, 0)
    length = jnp.broadcast_to(small[:, steps : steps + 1].astype(jnp.int32), grid)
    owner = jnp.zeros(grid, jnp.int32)
    filled = jnp.zeros(grid, jnp.int32)
    leads = jnp.zeros(grid, jnp.int32)
    for j in range(most):
        match = table[:, j : j + 1] == slot_id
        owner = jnp.where(match, request_id, owner)
        filled = jnp.where(match, jnp.clip(length - j * page, 0, page), filled)
        if j == 0:
            leads = jnp.where(match, request_id + 1, leads)
    owner = jnp.sum(owner.astype(F32), 0, keepdims=True).astype(jnp.int32) * steps
    filled = jnp.sum(filled.astype(F32), 0, keepdims=True).astype(jnp.int32)
    leads = jnp.sum(leads.astype(F32), 0, keepdims=True)
    spot = iota((1, page), 1)
    for s in range(slots):
        posown[:, s * page : (s + 1) * page] = jnp.where(
            spot < filled[:, s : s + 1], owner[:, s : s + 1], -8
        )
    rows_slot = slots * steps * heads
    leads = jnp.broadcast_to(leads, (8, 128)).astype(BF16)
    per_slot = steps * heads
    slot_of = (iota((rows_slot, 128), 0) // per_slot == iota((rows_slot, 128), 1)).astype(F32)
    leader = dot_nt(slot_of.astype(BF16), leads)[:, :1].astype(jnp.int32)
    row_step = (iota((rows_slot, 1), 0) // heads) % steps
    row_code = jnp.where(leader > 0, (leader - 1) * steps + row_step, -1)
    slot_of = (iota((128, rows_slot), 1) // per_slot == iota((128, rows_slot), 0)).astype(F32)
    leader = dot(leads, slot_of.astype(BF16))[:1].astype(jnp.int32)
    lane_step = (iota((1, rows_slot), 1) // heads) % steps
    lane_code = jnp.where(leader > 0, (leader - 1) * steps + lane_step, -1)
    pick[...] = jnp.where(row_code == iota((rows_slot, rows_all), 1), 1.0, 0.0).astype(BF16)
    put[...] = jnp.where(lane_code == iota((rows_all, rows_slot), 0), 1.0, 0.0).astype(BF16)
    home_put[...] = jnp.where(
        (lane_code >= 0) & (lane_code // rows_own == iota((n_seq, rows_slot), 0)), 1.0, 0.0
    ).astype(BF16)
    wanted = iota((rows_all, 1), 0)
    wanted = wanted % requests * steps + wanted // requests
    turn[...] = jnp.where(wanted == iota((rows_all, rows_all), 1), 1.0, 0.0).astype(BF16)

    pl.semaphore_wait(barrier, n_seq + n_ten - 2)
    all_to_all(0, True, send_a, recv_a)
    own_part = send_a[me].astype(F32)
    arrived(0, True, recv_a)
    residual = own_part + jnp.sum(recv_a[...].astype(F32), 0)
    res_own[...] = residual.astype(BF16)
    spread(1, False, res_own, res_all)
    res_all[mt] = residual.astype(BF16)
    arrived(1, False, res_all)
    normalise(res_all, g1_ref, b1_ref)

    def rotated(field):
        partner = jnp.where(
            first_half,
            pltpu.roll(field, cols - ROT // 2, 1),
            pltpu.roll(field, ROT // 2, 1),
        )
        return field * cos_wide + partner * sin_wide

    loads[1].wait()
    queries = rotated(dot(nrm[...], wq[...]) + qb_ref[...]).astype(BF16)
    q_own[...] = queries
    spread(2, True, q_own, q_all)
    q_all[me] = queries
    loads[2].wait()
    loads[3].wait()
    new_keys = rotated(dot(nrm[...], wk[...]) + kb_ref[...]).astype(BF16)
    new_values = (dot(nrm[...], wv[...]) + vb_ref[...]).astype(BF16)

    scale = HD**-0.5
    head_of = lane // HD
    q_tall = jnp.concatenate(
        [jnp.where(head_of == h, queries, jnp.zeros_like(queries)) for h in range(heads)], 0
    )
    tall = (heads * rows_own, rows_own)
    query_row = iota(tall, 0) % rows_own
    key_row = iota(tall, 1)
    seen = (query_row // steps == key_row // steps) & (key_row <= query_row)
    fresh = jnp.where(seen, dot_nt(q_tall, new_keys) * scale, NEGATIVE)
    fresh_top = jnp.max(fresh, -1, keepdims=True)
    fresh_weights = jnp.where(seen, jnp.exp(fresh - fresh_top), 0.0).astype(BF16)
    fresh_mass = jnp.sum(fresh_weights.astype(F32), -1, keepdims=True)
    fresh_mix = dot(fresh_weights, new_values)
    top_wide = jnp.zeros((rows_own, cols), F32)
    mass_wide = jnp.zeros((rows_own, cols), F32)
    mix_wide = jnp.zeros((rows_own, cols), F32)
    for h in range(heads):
        at = slice(h * rows_own, (h + 1) * rows_own)
        top_wide = jnp.where(head_of == h, fresh_top[at], top_wide)
        mass_wide = jnp.where(head_of == h, fresh_mass[at], mass_wide)
        mix_wide = jnp.where(head_of == h, fresh_mix[at], mix_wide)

    arrived(2, True, q_all)
    picked = dot(pick[...], q_all[...].reshape(rows_all, cols))
    row_head = iota((rows_slot, cols), 0) % heads
    own_head = row_head == iota((rows_slot, cols), 1) // HD
    q_rows[...] = jnp.where(own_head, picked, 0.0).astype(BF16)
    row_owner = row_code - row_step
    group = 4 if slots % 4 == 0 else 1
    span = group * page
    loads[4].wait()
    top = jnp.full((rows_slot, 1), NEGATIVE, F32)
    for g in range(slots // group):
        at = slice(g * span, (g + 1) * span)
        keys = kc[g * group : (g + 1) * group].reshape(span, cols)
        scores = dot_nt(q_rows[...], keys) * scale
        scores = jnp.where(row_owner == posown[:, at], scores, NEGATIVE)
        sbuf[:, at] = scores
        top = jnp.maximum(top, jnp.max(scores, -1, keepdims=True))
    loads[5].wait()
    mass = jnp.zeros((rows_slot, 1), F32)
    mix = jnp.zeros((rows_slot, cols), F32)
    for g in range(slots // group):
        at = slice(g * span, (g + 1) * span)
        weights = jnp.exp(sbuf[:, at] - top).astype(BF16)
        mass += jnp.sum(weights.astype(F32), -1, keepdims=True)
        mix += dot(weights, vc[g * group : (g + 1) * group].reshape(span, cols))
    level = top + jnp.log(mass)
    high = level.astype(BF16).astype(F32)
    middle = (level - high).astype(BF16).astype(F32)
    low = level - high - middle
    place = iota((rows_slot, 128), 1)
    here = place == (row_code % rows_own) * heads + iota((rows_slot, 128), 0) % heads
    levels = jnp.zeros((n_seq, 128), F32)
    for part in (high, middle, low):
        levels += dot(home_put[...], jnp.where(here, part, 0.0).astype(BF16))
    send_l[...] = levels.reshape(n_seq, 1, 128)
    all_to_all(8, True, send_l, recv_l)
    xbuf[...] = jnp.where(own_head, mix / mass, 0.0).astype(BF16)
    send_c[...] = dot(put[...], xbuf[...]).astype(BF16).reshape(n_seq, rows_own, cols)
    all_to_all(3, True, send_c, recv_c)
    own_level = send_l[me]
    arrived(8, True, recv_l)
    level_row = own_level + jnp.sum(recv_l[...], 0)
    place = iota((rows_own, 128), 1)
    start = iota((rows_own, 128), 0) * heads
    page_level = jnp.zeros((rows_own, cols), F32)
    for h in range(heads):
        value = jnp.sum(jnp.where(place == start + h, level_row, 0.0), -1, keepdims=True)
        page_level = jnp.where(head_of == h, value, page_level)
    own_part = send_c[me].astype(F32)
    arrived(3, True, recv_c)
    returned = own_part + jnp.sum(recv_c[...].astype(F32), 0)
    overall = jnp.maximum(page_level, top_wide)
    page_factor = jnp.exp(page_level - overall)
    fresh_factor = jnp.exp(top_wide - overall)
    attended = (returned * page_factor + mix_wide * fresh_factor) / (
        page_factor + mass_wide * fresh_factor
    )

    loads[6].wait()
    partial = dot(attended.astype(BF16), wo[...]).astype(BF16)
    for c in range(n_ten):
        send_e[c] = partial[:, c * cols : (c + 1) * cols]
    all_to_all(4, False, send_e, recv_e)
    own_part = send_e[mt].astype(F32)
    arrived(4, False, recv_e)
    attn_total = own_part + jnp.sum(recv_e[...].astype(F32), 0)
    hidden_one = (residual + attn_total).astype(BF16)
    h1_own[...] = hidden_one
    spread(5, False, h1_own, h1_all)
    h1_all[mt] = hidden_one
    arrived(5, False, h1_all)
    normalise(h1_all, g2_ref, b2_ref)
    loads[7].wait()
    loads[8].wait()
    gate = dot(nrm[...], wg[...])
    up = dot(nrm[...], wu[...])
    activated = (gate / (1.0 + jnp.exp(-gate)) * up).astype(BF16)
    loads[9].wait()
    partial = dot(activated, wd[...]).astype(BF16)
    for c in range(n_ten):
        send_h[c] = partial[:, c * cols : (c + 1) * cols]
    all_to_all(6, False, send_h, recv_h)
    own_part = send_h[mt].astype(F32)
    arrived(6, False, recv_h)
    mlp_total = own_part + jnp.sum(recv_h[...].astype(F32), 0)
    output = (hidden_one.astype(F32) + mlp_total).astype(BF16)
    out_own[...] = output
    spread(7, True, out_own, out_all)
    out_all[me] = output
    departed(0, True, recv_a)
    departed(1, False, res_all)
    departed(2, True, q_all)
    departed(3, True, recv_c)
    departed(8, True, recv_l)
    departed(4, False, recv_e)
    departed(5, False, h1_all)
    departed(6, False, recv_h)
    arrived(7, True, out_all)
    out_ref[...] = dot(turn[...], out_all[...].reshape(rows_all, cols)).astype(BF16)
    departed(7, True, out_all)


def shards(
    n_seq,
    n_ten,
    tokens,
    lengths,
    page_table,
    embedding,
    ln1_gain,
    ln1_bias,
    w_query,
    q_bias,
    w_key,
    k_bias,
    w_value,
    v_bias,
    w_out,
    ln2_gain,
    ln2_bias,
    w_gate,
    w_up,
    w_down,
    k_cache,
    v_cache,
):
    steps, requests = tokens.shape
    rows_all = steps * requests
    rows_own = rows_all // n_seq
    slots, page, cols = k_cache.shape
    heads = cols // HD
    width = n_ten * cols
    rows_slot = slots * steps * heads

    vmem = pl.BlockSpec(memory_space=pltpu.VMEM)
    hbm = pl.BlockSpec(memory_space=pl.ANY)
    scratch = lambda *shape: pltpu.VMEM(shape, BF16)
    out = pl.pallas_call(
        functools.partial(layer_kernel, n_seq, n_ten),
        out_shape=jax.ShapeDtypeStruct((rows_all, cols), BF16),
        in_specs=[vmem] * 10 + [hbm] * 10,
        out_specs=vmem,
        scratch_shapes=[
            scratch(*embedding.shape),
            scratch(*w_query.shape),
            scratch(*w_key.shape),
            scratch(*w_value.shape),
            scratch(*w_out.shape),
            scratch(*w_gate.shape),
            scratch(*w_up.shape),
            scratch(*w_down.shape),
            scratch(*k_cache.shape),
            scratch(*v_cache.shape),
            scratch(n_seq, rows_own, cols),
            scratch(n_seq - 1, rows_own, cols),
            scratch(rows_own, cols),
            scratch(n_ten, rows_own, cols),
            scratch(rows_own, width),
            scratch(rows_own, cols),
            scratch(n_seq, rows_own, cols),
            scratch(rows_slot, cols),
            pltpu.VMEM((rows_slot, slots * page), F32),
            scratch(rows_slot, cols),
            scratch(n_seq, rows_own, cols),
            scratch(n_seq - 1, rows_own, cols),
            pltpu.VMEM((n_seq, 1, 128), F32),
            pltpu.VMEM((n_seq - 1, 1, 128), F32),
            scratch(n_ten, rows_own, cols),
            scratch(n_ten - 1, rows_own, cols),
            scratch(rows_own, cols),
            scratch(n_ten, rows_own, cols),
            scratch(n_ten, rows_own, cols),
            scratch(n_ten - 1, rows_own, cols),
            scratch(rows_own, cols),
            scratch(n_seq, rows_own, cols),
            pltpu.VMEM((1, slots * page), jnp.int32),
            scratch(rows_slot, rows_all),
            scratch(rows_all, rows_slot),
            scratch(n_seq, rows_slot),
            scratch(rows_all, rows_all),
            pltpu.SemaphoreType.DMA((10,)),
            pltpu.SemaphoreType.DMA((9,)),
            pltpu.SemaphoreType.DMA((9,)),
        ],
        compiler_params=pltpu.CompilerParams(
            collective_id=0, has_side_effects=True, vmem_limit_bytes=62 * 1024 * 1024
        ),
        name="layer",
    )(
        tokens,
        lengths[None],
        page_table.T,
        ln1_gain[None],
        ln1_bias[None],
        q_bias[None],
        k_bias[None],
        v_bias[None],
        ln2_gain[None],
        ln2_bias[None],
        embedding,
        w_query,
        w_key,
        w_value,
        w_out,
        w_gate,
        w_up,
        w_down,
        k_cache,
        v_cache,
    )
    return out.reshape(steps, requests, cols)


def solution(mesh):
    placed = (
        P(),
        P(),
        P(),
        P("seq", "tensor"),
        P(),
        P(),
        P(None, "tensor"),
        P("tensor"),
        P(None, "tensor"),
        P("tensor"),
        P(None, "tensor"),
        P("tensor"),
        P("tensor", None),
        P(),
        P(),
        P(None, "tensor"),
        P(None, "tensor"),
        P("tensor", None),
        P("seq", None, "tensor"),
        P("seq", None, "tensor"),
    )
    return jax.shard_map(
        functools.partial(shards, mesh.shape["seq"], mesh.shape["tensor"]),
        mesh=mesh,
        in_specs=placed,
        out_specs=P(None, None, "tensor"),
        check_vma=False,
    )
```
